32 devices in a mesh: dp: 16 (over z, x, core), tensor: 2 (over y).
Axes of the slice: x: 2, y: 2, z: 4, core: 2. Of those that a mesh axis runs over, the one named last changes fastest.
Arguments:
- tokens: bfloat16 [16384, 1024], P(('dp', 'tensor')), may hold values from -6 to 6
- norm_gain1: float32 [1024], replicated, may hold values from 0.5 to 1.5
- w_query: bfloat16 [1024, 1024], P('dp', 'tensor'), may hold values from -0.1875 to 0.1875
- w_key: bfloat16 [1024, 1024], P('dp', 'tensor'), may hold values from -0.1875 to 0.1875
- w_value: bfloat16 [1024, 2048], P('dp', 'tensor'), may hold values from -0.1875 to 0.1875
- w_gate: bfloat16 [1024, 2048], P('dp', 'tensor'), may hold values from -0.1875 to 0.1875
- w_decay: bfloat16 [1024, 8], P('dp', 'tensor'), may hold values from -0.375 to 0.375
- w_write: bfloat16 [1024, 8], P('dp', 'tensor'), may hold values from -0.375 to 0.375
- conv_query: float32 [4, 1024], P(None, 'tensor'), may hold values from -3 to 3
- conv_key: float32 [4, 1024], P(None, 'tensor'), may hold values from -3 to 3
- conv_value: float32 [4, 2048], P(None, 'tensor'), may hold values from -3 to 3
- a_log: float32 [8], P('tensor'), may hold values from -3 to 1
- dt_bias: float32 [8], P('tensor'), may hold values from -4 to -1
- out_gain: float32 [256], replicated, may hold values from 0.5 to 1.5
- w_out: bfloat16 [2048, 1024], P('tensor', 'dp'), may hold values from -0.25 to 0.25
- norm_gain2: float32 [1024], replicated, may hold values from 0.5 to 1.5
- w_ffgate: bfloat16 [1024, 2816], P('dp', 'tensor'), may hold values from -0.1875 to 0.1875
- w_ffup: bfloat16 [1024, 2816], P('dp', 'tensor'), may hold values from -0.1875 to 0.1875
- w_ffdown: bfloat16 [2816, 1024], P('tensor', 'dp'), may hold values from -0.109375 to 0.109375
- cotangent: bfloat16 [16384, 1024], P(('dp', 'tensor')), may hold values from -11 to 11, as said below
Outputs:
- result: bfloat16 [16384, 1024], P(('dp', 'tensor'))
- grad_tokens: float32 [16384, 1024], P(('dp', 'tensor'))
- grad_norm_gain1: float32 [1024], replicated
- grad_query: float32 [1024, 1024], P('dp', 'tensor')
- grad_key: float32 [1024, 1024], P('dp', 'tensor')
- grad_value: float32 [1024, 2048], P('dp', 'tensor')
- grad_gate: float32 [1024, 2048], P('dp', 'tensor')
- grad_decay: float32 [1024, 8], P('dp', 'tensor')
- grad_write: float32 [1024, 8], P('dp', 'tensor')
- grad_conv_query: float32 [4, 1024], P(None, 'tensor')
- grad_conv_key: float32 [4, 1024], P(None, 'tensor')
- grad_conv_value: float32 [4, 2048], P(None, 'tensor')
- grad_a_log: float32 [8], P('tensor')
- grad_dt_bias: float32 [8], P('tensor')
- grad_out_gain: float32 [256], replicated
- grad_out: float32 [2048, 1024], P('tensor', 'dp')
- grad_norm_gain2: float32 [1024], replicated
- grad_ffgate: float32 [1024, 2816], P('dp', 'tensor')
- grad_ffup: float32 [1024, 2816], P('dp', 'tensor')
- grad_ffdown: float32 [2816, 1024], P('tensor', 'dp')
The draws below stay inside these ranges and needn't reach their ends.
Inputs may be any that keep to these rules, and one draw needn't show every extreme that they name: `cotangent`: gradient of the loss, of order one in every row.
All inputs are finite; a program needn't handle non-finite values.
Results may differ from the reference program's by a relative error of at most 0.012.
Values may be sent and summed in bfloat16 or wider, within the bound.
No kernel may reach another device: no remote copies, remote signals or barrier semaphores. Data moves between devices by JAX's collectives and lax.ppermute only.
A program may use at most 256 MiB of HBM per device.

```python
import math
import jax
import jax.numpy as jnp
from jax import lax

D = 1024
H = 8
DK = 128
DV = 256
FF = 2816
KW = 4
SPAN = 64
LEN = 512
TOKENS = 16384


def draw_cotangent(key, part):
    row_pos = jnp.arange(TOKENS, dtype=jnp.float32)[:, None] / (TOKENS - 1)
    sampled = jnp.clip(jax.random.normal(key, (TOKENS, D), jnp.float32), -6.0, 6.0)
    factor = 3.0 ** row_pos / 1.7
    return (sampled * factor).astype(jnp.bfloat16)


def block_scale(stream_key, dims, cuts, smallest, largest):
    loudness, own = 1.0, jax.random.fold_in(stream_key, 6)
    for axis_at, shards_of in cuts:
        heights = jnp.exp(jax.random.uniform(jax.random.fold_in(own, axis_at), (shards_of,), jnp.float32, smallest / len(cuts), largest / len(cuts)))
        loudness = loudness * jnp.repeat(heights, dims[axis_at] // shards_of).reshape([-1 if axis == axis_at else 1 for axis in range(len(dims))])
    return loudness


def centred(own_key, dims, spread, limit, cuts=(), kind=jnp.bfloat16):
    level = block_scale(own_key, dims, cuts, -0.22, 0.18) if cuts else 1.0
    values = jax.random.normal(own_key, dims, jnp.float32) * spread * level
    return jnp.minimum(jnp.maximum(values, -limit), limit).astype(kind)


def setup_inputs(seed: int = 0) -> dict:
    seeds = jax.random.split(jax.random.key(seed), 21)
    tokens = centred(seeds[0], (TOKENS, D), 1.0, 6.0, ((0, 32),))
    norm_gain1 = jnp.clip(1.0 + 0.1 * jax.random.normal(seeds[1], (D,), jnp.float32), 0.5, 1.5)
    w_query = centred(seeds[2], (D, H * DK), D ** -0.5, 0.1875, ((0, 16), (1, 2)))
    w_key = centred(seeds[3], (D, H * DK), D ** -0.5, 0.1875, ((0, 16), (1, 2)))
    w_value = centred(seeds[4], (D, H * DV), D ** -0.5, 0.1875, ((0, 16), (1, 2)))
    w_gate = centred(seeds[5], (D, H * DV), D ** -0.5, 0.1875, ((0, 16), (1, 2)))
    w_decay = centred(seeds[6], (D, H), (D // 4) ** -0.5, 0.375, ((0, 16), (1, 2)))
    w_write = centred(seeds[7], (D, H), (D // 4) ** -0.5, 0.375, ((0, 16), (1, 2)))
    conv_query = centred(seeds[8], (KW, H * DK), KW ** -0.5, 3.0, ((1, 2),), jnp.float32)
    conv_key = centred(seeds[9], (KW, H * DK), KW ** -0.5, 3.0, ((1, 2),), jnp.float32)
    conv_value = centred(seeds[10], (KW, H * DV), KW ** -0.5, 3.0, ((1, 2),), jnp.float32)
    a_log = jnp.clip(-3.0 + 4.0 * jax.random.uniform(seeds[11], (H,), jnp.float32) ** block_scale(seeds[11], (H,), ((0, 2),), -0.2, 0.2), -3.0, 1.0)
    dt_bias = jnp.clip(-4.0 + 3.0 * jax.random.uniform(seeds[12], (H,), jnp.float32) ** block_scale(seeds[12], (H,), ((0, 2),), -0.2, 0.2), -4.0, -1.0)
    out_gain = jnp.clip(1.0 + 0.1 * jax.random.normal(seeds[13], (DV,), jnp.float32), 0.5, 1.5)
    w_out = centred(seeds[14], (H * DV, D), (H * DV // 4) ** -0.5, 0.25, ((0, 2), (1, 16)))
    norm_gain2 = jnp.clip(1.0 + 0.1 * jax.random.normal(seeds[15], (D,), jnp.float32), 0.5, 1.5)
    w_ffgate = centred(seeds[16], (D, FF), D ** -0.5, 0.1875, ((0, 16), (1, 2)))
    w_ffup = centred(seeds[17], (D, FF), D ** -0.5, 0.1875, ((0, 16), (1, 2)))
    w_ffdown = centred(seeds[18], (FF, D), FF ** -0.5, 0.109375, ((0, 2), (1, 16)))
    cotangent = draw_cotangent(jax.random.fold_in(seeds[20], 71), 0)
    return {"tokens": tokens, "norm_gain1": norm_gain1, "w_query": w_query, "w_key": w_key, "w_value": w_value, "w_gate": w_gate, "w_decay": w_decay, "w_write": w_write, "conv_query": conv_query, "conv_key": conv_key, "conv_value": conv_value, "a_log": a_log, "dt_bias": dt_bias, "out_gain": out_gain, "w_out": w_out, "norm_gain2": norm_gain2, "w_ffgate": w_ffgate, "w_ffup": w_ffup, "w_ffdown": w_ffdown, "cotangent": cotangent}


@jax.custom_vjp
def low(v):
    return lax.optimization_barrier(v.astype(jnp.bfloat16)).astype(jnp.float32)

@jax.custom_vjp
def low_back(v):
    return v

def low_keep(v):
    return (low(v), None)

def low_pass(kept, grad):
    return (grad,)

def back_keep(v):
    return (v, None)

def back_low(kept, grad):
    return (low(grad),)
low.defvjp(low_keep, low_pass)
low_back.defvjp(back_keep, back_low)

def row_norm(values, gain):
    factor = lax.rsqrt(lax.optimization_barrier(jnp.mean(values * values, axis=-1, keepdims=True)) + 1e-05)
    return values * factor * gain

def unit_norm(vectors):
    return vectors * lax.rsqrt(lax.optimization_barrier(jnp.sum(vectors * vectors, axis=-1, keepdims=True)) + 1e-06)

def causal_conv(values, kernel):
    taps_count = kernel.shape[0]
    seq_len = values.shape[1]
    padded = jnp.pad(values, ((0, 0), (taps_count - 1, 0), (0, 0)))
    summed = padded[:, 0:seq_len, :] * kernel[0]
    for offset in range(1, taps_count):
        summed = summed + padded[:, offset:offset + seq_len, :] * kernel[offset]
    return summed

def to_blocks(tensor, seq_count, nblocks):
    heads_n = tensor.shape[2]
    return jnp.transpose(tensor.reshape(seq_count, nblocks, SPAN, heads_n, -1), (0, 3, 1, 2, 4))

def delta_rule(queries, keys_in, values_in, decay, write_rate):
    highest = lax.Precision.HIGHEST
    seq_count, seq_len, heads_n, key_dim = queries.shape
    val_dim = values_in.shape[-1]
    nblocks = seq_len // SPAN
    q_blk = to_blocks(queries, seq_count, nblocks)
    k_blk = to_blocks(keys_in, seq_count, nblocks)
    v_blk = to_blocks(values_in, seq_count, nblocks)
    g_blk = to_blocks(decay[..., None], seq_count, nblocks)[..., 0]
    b_blk = to_blocks(write_rate[..., None], seq_count, nblocks)[..., 0]
    cumul = jnp.cumsum(g_blk, axis=-1)
    positions = jnp.arange(SPAN)
    strict = positions[:, None] > positions[None, :]
    inclusive = positions[:, None] >= positions[None, :]
    cum_gaps = cumul[..., :, None] - cumul[..., None, :]
    strict_decay = jnp.where(strict, jnp.exp(jnp.where(strict, cum_gaps, 0.0)), 0.0)
    incl_decay = jnp.where(inclusive, jnp.exp(jnp.where(inclusive, cum_gaps, 0.0)), 0.0)
    key_inner = jnp.einsum('shnik,shnjk->shnij', k_blk, k_blk, precision=highest)
    system = jnp.eye(SPAN, dtype=jnp.float32) + b_blk[..., :, None] * key_inner * strict_decay
    right_side = jnp.concatenate([b_blk[..., None] * v_blk, (b_blk * jnp.exp(cumul))[..., None] * k_blk], axis=-1)
    solved = jax.scipy.linalg.solve_triangular(system, right_side, lower=True, unit_diagonal=True)
    solved_v = solved[..., :val_dim]
    solved_k = solved[..., val_dim:]
    query_key = jnp.einsum('shnik,shnjk->shnij', q_blk, k_blk, precision=highest) * incl_decay
    query_dec = q_blk * jnp.exp(cumul)[..., None]
    key_dec = k_blk * jnp.exp(cumul[..., -1:] - cumul)[..., None]
    last_dec = jnp.exp(cumul[..., -1])

    def advance(carried, pieces):
        part_v, part_k, part_qk, part_q, part_kd, part_last = pieces
        update = part_v - jnp.einsum('shck,shkv->shcv', part_k, carried, precision=highest)
        output = jnp.einsum('shck,shkv->shcv', part_q, carried, precision=highest)
        output = output + jnp.einsum('shcj,shjv->shcv', part_qk, update, precision=highest)
        carried = part_last[..., None, None] * carried + jnp.einsum('shck,shcv->shkv', part_kd, update, precision=highest)
        return (carried, output)
    inputs = tuple((jnp.moveaxis(member, 2, 0) for member in (solved_v, solved_k, query_key, query_dec, key_dec, last_dec)))
    initial = jnp.zeros((seq_count, heads_n, key_dim, val_dim), jnp.float32)
    unused, outputs = lax.scan(jax.checkpoint(advance), initial, inputs)
    return jnp.transpose(outputs, (1, 0, 3, 2, 4)).reshape(seq_count, seq_len, heads_n, val_dim)

def mix_heads(proj_q, proj_k, proj_v, proj_gate, proj_decay, proj_write, conv_q, conv_k, conv_v, a_log, dt_bias, out_gain):
    row_count = proj_q.shape[0]
    seq_count = row_count // LEN
    heads_n = proj_decay.shape[1]

    def conv_act(projected, kernel):
        convolved = causal_conv(projected.reshape(seq_count, LEN, -1), kernel)
        return jax.nn.silu(convolved).reshape(seq_count, LEN, heads_n, -1)
    queries = unit_norm(conv_act(proj_q, conv_q))
    queries = queries * (1.0 / math.sqrt(queries.shape[-1]))
    keys_in = unit_norm(conv_act(proj_k, conv_k))
    values_in = conv_act(proj_v, conv_v)
    write_rate = jax.nn.sigmoid(proj_write).reshape(seq_count, LEN, heads_n)
    decay = (-jnp.exp(a_log) * jax.nn.softplus(proj_decay + dt_bias)).reshape(seq_count, LEN, heads_n)
    mixed = delta_rule(queries, keys_in, values_in, decay, write_rate)
    normed = row_norm(mixed, out_gain)
    gated = normed * jax.nn.silu(proj_gate.reshape(seq_count, LEN, heads_n, -1))
    return low(gated.reshape(row_count, -1))

def matmul_high(left, right):
    return jnp.dot(left.astype(jnp.float32), right.astype(jnp.float32), precision=lax.Precision.HIGHEST, preferred_element_type=jnp.float32)

def layer(tokens, norm_gain1, w_query, w_key, w_value, w_gate, w_decay, w_write, conv_query, conv_key, conv_value, a_log, dt_bias, out_gain, w_out, norm_gain2, w_ffgate, w_ffup, w_ffdown):
    normed1 = low(row_norm(tokens, norm_gain1))

    def project(weight):
        return low_back(matmul_high(normed1, weight))
    gated = mix_heads(project(w_query), project(w_key), project(w_value), project(w_gate), project(w_decay), project(w_write), conv_query, conv_key, conv_value, a_log, dt_bias, out_gain)
    resid1 = tokens + low_back(matmul_high(gated, w_out))
    normed2 = low(row_norm(resid1, norm_gain2))
    gate_val = low_back(matmul_high(normed2, w_ffgate))
    up_val = low_back(matmul_high(normed2, w_ffup))
    hidden = low(jax.nn.silu(gate_val) * up_val)
    return resid1 + low_back(matmul_high(hidden, w_ffdown))

def reference(tokens, norm_gain1, w_query, w_key, w_value, w_gate, w_decay, w_write, conv_query, conv_key, conv_value, a_log, dt_bias, out_gain, w_out, norm_gain2, w_ffgate, w_ffup, w_ffdown, cotangent):
    seq_total = TOKENS // LEN
    group_seqs = max((count for count in range(1, 9) if seq_total % count == 0))
    nsteps = seq_total // group_seqs
    params = tuple((member.astype(jnp.float32) for member in (norm_gain1, w_query, w_key, w_value, w_gate, w_decay, w_write, conv_query, conv_key, conv_value, a_log, dt_bias, out_gain, w_out, norm_gain2, w_ffgate, w_ffup, w_ffdown)))
    token_groups = tokens.astype(jnp.float32).reshape(nsteps, group_seqs * LEN, D)
    cot_groups = cotangent.astype(jnp.float32).reshape(nsteps, group_seqs * LEN, D)

    def one_group(totals, pieces):
        token_part, cot_part = pieces
        output, pullback = jax.vjp(layer, token_part, *params)
        grads = pullback(cot_part)
        new_totals = tuple((earlier + extra for earlier, extra in zip(totals, grads[1:])))
        return (new_totals, (output.astype(jnp.bfloat16), grads[0]))
    zeros = tuple((jnp.zeros_like(member) for member in params))
    totals, (outputs, token_grads) = lax.scan(one_group, zeros, (token_groups, cot_groups))
    return (outputs.reshape(TOKENS, D), token_grads.reshape(TOKENS, D), totals[0], totals[1], totals[2], totals[3], totals[4], totals[5], totals[6], totals[7], totals[8], totals[9], totals[10], totals[11], totals[12], totals[13], totals[14], totals[15], totals[16], totals[17])
```

```python
import math, functools
import jax, jax.numpy as jnp
from jax import lax
from jax.experimental import pallas as pl
from jax.experimental.pallas import tpu as pltpu
from jax.sharding import PartitionSpec as P

F32 = jnp.float32
BF16 = jnp.bfloat16
LEN = 512
DK = 128
DV = 256
CHUNK = 128
PARTS = LEN // CHUNK


def dot_nn(a, b):
    return lax.dot_general(a, b, (((1,), (0,)), ((), ())), preferred_element_type=F32)


def dot_nt(a, b):
    return lax.dot_general(a, b, (((1,), (1,)), ((), ())), preferred_element_type=F32)


def dot_tn(a, b):
    return lax.dot_general(a, b, (((0,), (0,)), ((), ())), preferred_element_type=F32)


def sigmoid(x):
    return 1.0 / (1.0 + jnp.exp(-x))


def softplus(x):
    return jnp.maximum(x, 0.0) + jnp.log1p(jnp.exp(-jnp.abs(x)))


def split3(x):
    first = x.astype(BF16)
    rest = x - first.astype(F32)
    second = rest.astype(BF16)
    third = (rest - second.astype(F32)).astype(BF16)
    return first, second, third


def exact_sum(ones, x, pieces):
    parts = split3(x)[:pieces]
    total = dot_nn(ones, parts[0])
    for part in parts[1:]:
        total = total + dot_nn(ones, part)
    return total


def iota2(rows, cols, axis):
    return lax.broadcasted_iota(jnp.int32, (rows, cols), axis)


def same_group(size):
    shift = size.bit_length() - 1
    return (iota2(CHUNK, CHUNK, 0) >> shift) == (iota2(CHUNK, CHUNK, 1) >> shift)


def invert_all(lowers):
    row, col = iota2(CHUNK, CHUNK, 0), iota2(CHUNK, CHUNK, 1)
    eye = jnp.where(row == col, 1.0, 0.0)
    in8 = same_group(8)
    base = [jnp.where(in8, lower, 0.0) for lower in lowers]
    base_low = [member.astype(BF16) for member in base]
    second = [dot_nn(member, member) for member in base_low]
    second_low = [member.astype(BF16) for member in second]
    third = [dot_nn(a, b) for a, b in zip(base_low, second_low)]
    fourth = [dot_nn(member, member).astype(BF16) for member in second_low]
    start = [eye - a + b - c for a, b, c in zip(base, second, third)]
    inverse = [a + dot_nn(a.astype(BF16), b) for a, b in zip(start, fourth)]
    size = 8
    while size < CHUNK:
        ring = same_group(2 * size) & jnp.logical_not(same_group(size))
        between = [jnp.where(ring, lower, 0.0).astype(BF16) for lower in lowers]
        low = [member.astype(BF16) for member in inverse]
        inner = [dot_nn(a, b).astype(BF16) for a, b in zip(between, low)]
        inverse = [a - dot_nn(b, c) for a, b, c in zip(inverse, low, inner)]
        size *= 2
    return [member.astype(BF16) for member in inverse]


def window(ref, part, halo=8):
    body = ref[pl.ds(part * CHUNK, CHUNK), :].astype(F32)
    if part == 0:
        head = jnp.zeros((halo, body.shape[1]), F32)
    else:
        head = ref[pl.ds(part * CHUNK - halo, halo), :].astype(F32)
    return jnp.concatenate([head, body], axis=0)


def shifted(rows, tap):
    return rows[5 + tap : 5 + tap + CHUNK, :]


def convolve(rows, taps):
    total = shifted(rows, 0) * taps[0:1, :]
    for tap in range(1, 4):
        total = total + shifted(rows, tap) * taps[tap : tap + 1, :]
    return total


def pick(rows, lane):
    cols = lax.broadcasted_iota(jnp.int32, rows.shape, 1)
    return jnp.sum(jnp.where(cols == lane, rows, 0.0), axis=1, keepdims=True)


def chunk_rates(ab_ref, heads_ref, part, head, heads_n):
    rows = ab_ref[pl.ds(part * CHUNK, CHUNK), :].astype(F32)
    decay_in = pick(rows, head) + pick(heads_ref[1:2, :], head)
    write = sigmoid(pick(rows, heads_n + head))
    rate = -jnp.exp(pick(heads_ref[0:1, :], head))
    soft = softplus(decay_in)
    decay = jnp.broadcast_to(rate * soft, (CHUNK, CHUNK))
    lower = (iota2(CHUNK, CHUNK, 0) >= iota2(CHUNK, CHUNK, 1)).astype(F32).astype(BF16)
    total = exact_sum(lower, decay, 3)
    return write, total, decay_in, rate, soft


def chunk_core(q_ref, k_ref, v_ref, ab_ref, heads_ref, cq, ck, cv, part, head, heads_n):
    row, col = iota2(CHUNK, CHUNK, 0), iota2(CHUNK, CHUNK, 1)
    strict, inclusive = row > col, row >= col
    out = {}
    write, total, decay_in, rate, soft = chunk_rates(ab_ref, heads_ref, part, head, heads_n)
    out.update(write=write, decay_in=decay_in, rate=rate, soft=soft)
    rows_q, rows_k, rows_v = window(q_ref, part), window(k_ref, part), window(v_ref, part)
    xq, xk, xv = convolve(rows_q, cq), convolve(rows_k, ck), convolve(rows_v, cv)
    gq, gk, gv = sigmoid(xq), sigmoid(xk), sigmoid(xv)
    sq, sk, values = xq * gq, xk * gk, xv * gv
    rq = lax.rsqrt(jnp.sum(sq * sq, axis=1, keepdims=True) + 1e-06)
    rk = lax.rsqrt(jnp.sum(sk * sk, axis=1, keepdims=True) + 1e-06)
    queries = sq * rq * (1.0 / math.sqrt(DK))
    keys = sk * rk
    q_low, k_low = queries.astype(BF16), keys.astype(BF16)
    gaps = jnp.minimum(total - total.T, 0.0)
    fade = jnp.where(inclusive, jnp.exp(gaps), 0.0)
    fade_strict = jnp.where(strict, fade, 0.0)
    key_inner = dot_nt(k_low, k_low)
    scores = dot_nt(q_low, k_low) * fade
    from_start = jnp.exp(total)
    to_end = jnp.exp(total[CHUNK - 1 : CHUNK, :] - total)
    last = jnp.exp(total[CHUNK - 1 : CHUNK, 0:1])
    lower = write * key_inner * fade_strict
    out.update(rows_q=rows_q, rows_k=rows_k, rows_v=rows_v, xq=xq, xk=xk, xv=xv, gq=gq, gk=gk, gv=gv)
    out.update(rq=rq, rk=rk, queries=queries, keys=keys, values=values, q_low=q_low, k_low=k_low)
    out.update(fade=fade, fade_strict=fade_strict, key_inner=key_inner, scores=scores, lower=lower)
    out.update(from_start=from_start, to_end=to_end, last=last)
    out.update(key_start=(write * from_start) * keys, q_start=queries * from_start, key_end=keys * to_end)
    return out


def forward_kernel(heads_n, q_ref, k_ref, v_ref, g_ref, ab_ref, cq_ref, ck_ref, cv_ref, heads_ref, gain_ref,
                   gated_ref, mixed_ref, delta_ref, solve_ref, state_ref):
    head = pl.program_id(1)
    cq, ck, cv, gain = cq_ref[...], ck_ref[...], cv_ref[...], gain_ref[0:1, :]
    cores = [
        chunk_core(q_ref, k_ref, v_ref, ab_ref, heads_ref, cq, ck, cv, part, head, heads_n)
        for part in range(PARTS)
    ]
    solves = invert_all([core["lower"] for core in cores])
    for part in range(PARTS):
        solve_ref[0, 0, part] = solves[part]
    value_parts = [dot_nn(t, (c["write"] * c["values"]).astype(BF16)) for t, c in zip(solves, cores)]
    key_parts = [dot_nn(t, c["key_start"].astype(BF16)).astype(BF16) for t, c in zip(solves, cores)]
    state = jnp.zeros((DK, DV), F32)
    for part in range(PARTS):
        core = cores[part]
        state_low = state.astype(BF16)
        state_ref[0, 0, part] = state_low
        update = value_parts[part] - dot_nn(key_parts[part], state_low)
        update_low = update.astype(BF16)
        mixed = dot_nn(core["q_start"].astype(BF16), state_low) + dot_nn(core["scores"].astype(BF16), update_low)
        if part < PARTS - 1:
            state = core["last"] * state + dot_tn(core["key_end"].astype(BF16), update_low)
        span = pl.ds(part * CHUNK, CHUNK)
        delta_ref[span, :] = update_low
        mixed_ref[span, :] = mixed.astype(BF16)
        factor = lax.rsqrt(jnp.mean(mixed * mixed, axis=1, keepdims=True) + 1e-05)
        gate_in = g_ref[span, :].astype(F32)
        gated_ref[span, :] = (mixed * factor * gain * (gate_in * sigmoid(gate_in))).astype(BF16)


def backward_kernel(heads_n, q_ref, k_ref, v_ref, g_ref, ab_ref, cq_ref, ck_ref, cv_ref, heads_ref, gain_ref,
                    grad_ref, mixed_ref, delta_ref, solve_ref, state_ref, dp_ref, small_ref, ab_acc):
    head = pl.program_id(1)
    row, col = iota2(CHUNK, CHUNK, 0), iota2(CHUNK, CHUNK, 1)
    strict = row > col
    upper_ones = (row <= col).astype(F32).astype(BF16)
    cq, ck, cv, gain = cq_ref[...], ck_ref[...], cv_ref[...], gain_ref[0:1, :]
    width_k, width_v = heads_n * DK, heads_n * DV
    scale = 1.0 / math.sqrt(DK)

    def fold(x):
        return jnp.sum(x.reshape(CHUNK // 8, 8, x.shape[1]), axis=0)

    state_grad = jnp.zeros((DK, DV), F32)
    gain_sum = jnp.zeros((8, DV), F32)
    taps_sum = {name: [jnp.zeros((8, size), F32) for _ in range(4)] for name, size in (("q", DK), ("k", DK), ("v", DV))}
    heads_next = {"q": jnp.zeros((8, DK), F32), "k": jnp.zeros((8, DK), F32), "v": jnp.zeros((8, DV), F32)}
    rate_sum = jnp.zeros((8, CHUNK), F32)
    bias_sum = jnp.zeros((8, CHUNK), F32)
    for part in reversed(range(PARTS)):
        core = chunk_core(q_ref, k_ref, v_ref, ab_ref, heads_ref, cq, ck, cv, part, head, heads_n)
        span = pl.ds(part * CHUNK, CHUNK)
        write, keys, queries, values = core["write"], core["keys"], core["queries"], core["values"]
        k_low, q_low, fade = core["k_low"], core["q_low"], core["fade"]
        solve, state_low, delta = solve_ref[0, 0, part], state_ref[0, 0, part], delta_ref[span, :]
        mixed = mixed_ref[span, :].astype(F32)
        factor = lax.rsqrt(jnp.mean(mixed * mixed, axis=1, keepdims=True) + 1e-05)
        normed = mixed * factor
        gate_in = g_ref[span, :].astype(F32)
        gate_sig = sigmoid(gate_in)
        gate = gate_in * gate_sig
        grad = grad_ref[span, :].astype(F32)
        plain = grad * normed
        gain_sum = gain_sum + fold(plain * gate)
        dp_ref[span, pl.ds(pl.multiple_of(2 * width_k + width_v + head * DV, DV), DV)] = (
            plain * gain * (gate_sig + gate * (1.0 - gate_sig))
        ).astype(BF16)
        normed_grad = grad * gate * gain
        mixed_grad = factor * (normed_grad - normed * jnp.mean(normed_grad * normed, axis=1, keepdims=True))
        mixed_low = mixed_grad.astype(BF16)
        key_part = dot_nn(solve, core["key_start"].astype(BF16)).astype(BF16)
        grad_low = state_grad.astype(BF16)
        update_grad = dot_tn(core["scores"].astype(BF16), mixed_low) + dot_nn(core["key_end"].astype(BF16), grad_low)
        update_low = update_grad.astype(BF16)
        key_end_grad = dot_nt(delta, grad_low)
        last_grad = jnp.sum(state_low.astype(F32) * state_grad)
        if part > 0:
            state_grad = (
                core["last"] * state_grad
                + dot_tn(core["q_start"].astype(BF16), mixed_low)
                - dot_tn(key_part, update_low)
            )
        q_start_grad = dot_nt(mixed_low, state_low)
        scores_grad = dot_nt(mixed_low, delta)
        right_grad = dot_tn(solve, update_low)
        right_low = right_grad.astype(BF16)
        lower_grad = jnp.where(strict, -dot_nt(right_low, delta), 0.0)
        key_start_grad = -dot_nt(right_low, state_low)
        inner_low = (scores_grad * fade).astype(BF16)
        queries_grad = q_start_grad * core["from_start"] + dot_nn(inner_low, k_low)
        faded_lower = lower_grad * core["fade_strict"]
        key_inner_grad = write * faded_lower
        both = (key_inner_grad + key_inner_grad.T).astype(BF16)
        keys_grad = (
            key_end_grad * core["to_end"]
            + key_start_grad * (write * core["from_start"])
            + dot_tn(inner_low, q_low)
            + dot_nn(both, k_low)
        )
        values_grad = write * right_grad
        start_keys = key_start_grad * core["from_start"] * keys
        write_grad = (
            jnp.sum(right_grad * values, axis=1, keepdims=True)
            + jnp.sum(start_keys + faded_lower * core["key_inner"], axis=1, keepdims=True)
        )
        ends = key_end_grad * core["key_end"]
        gaps_grad = scores_grad * core["scores"] + lower_grad * core["lower"]
        total_grad = jnp.sum(
            q_start_grad * core["q_start"] + write * start_keys - ends + gaps_grad - gaps_grad.T, axis=1, keepdims=True
        )
        at_end = jnp.sum(ends) + last_grad * core["last"]
        decay_grad = exact_sum(upper_ones, jnp.broadcast_to(total_grad, (CHUNK, CHUNK)), 2) + at_end
        rate_sum = rate_sum + fold(decay_grad * (core["rate"] * core["soft"]))
        decay_in_grad = decay_grad * (core["rate"] * sigmoid(core["decay_in"]))
        bias_sum = bias_sum + fold(decay_in_grad)
        write_in_grad = write_grad * (write * (1.0 - write))
        entry = jnp.where(col == head, decay_in_grad, 0.0) + jnp.where(col == heads_n + head, write_in_grad, 0.0)

        @pl.when(head == 0)
        def _():
            ab_acc[span, :] = entry

        @pl.when(head > 0)
        def _():
            ab_acc[span, :] = ab_acc[span, :] + entry

        unit_grad = queries_grad * scale
        unit = queries * (1.0 / scale)
        sq_grad = core["rq"] * (unit_grad - unit * jnp.sum(unit_grad * unit, axis=1, keepdims=True))
        sk_grad = core["rk"] * (keys_grad - keys * jnp.sum(keys_grad * keys, axis=1, keepdims=True))
        for name, grad_in, x, sig, rows, taps, start, size in (
            ("q", sq_grad, core["xq"], core["gq"], core["rows_q"], cq, 0, DK),
            ("k", sk_grad, core["xk"], core["gk"], core["rows_k"], ck, width_k, DK),
            ("v", values_grad, core["xv"], core["gv"], core["rows_v"], cv, 2 * width_k, DV),
        ):
            x_grad = grad_in * (sig + x * sig * (1.0 - sig))
            for tap in range(4):
                taps_sum[name][tap] = taps_sum[name][tap] + fold(shifted(rows, tap) * x_grad)
            longer = jnp.concatenate([x_grad, heads_next[name]], axis=0)
            heads_next[name] = x_grad[0:8, :]
            proj = x_grad * taps[3:4, :]
            for tap in range(3):
                proj = proj + longer[3 - tap : 3 - tap + CHUNK, :] * taps[tap : tap + 1, :]
            dp_ref[span, pl.ds(pl.multiple_of(start + head * size, size), size)] = proj.astype(BF16)

    @pl.when(head == heads_n - 1)
    def _():
        dp_ref[:, pl.ds(2 * width_k + 2 * width_v, 128)] = ab_acc[...].astype(BF16)

    def row(x):
        return jnp.sum(x, axis=0, keepdims=True)

    lane = iota2(1, DV, 1)
    rates = jnp.sum(rate_sum[:, 0:1], axis=0, keepdims=True)
    biases = jnp.sum(bias_sum[:, 0:1], axis=0, keepdims=True)
    small = [row(taps_sum["v"][tap]) for tap in range(4)]
    small += [jnp.concatenate([row(taps_sum["q"][tap]), row(taps_sum["k"][tap])], axis=1) for tap in range(4)]
    small += [row(gain_sum), jnp.where(lane == 0, rates, 0.0) + jnp.where(lane == 1, biases, 0.0)]
    small += [jnp.zeros((6, DV), F32)]
    small_ref[0, 0] = jnp.concatenate(small, axis=0)


def specs(heads_n):
    col_v = 2 * heads_n * DK // DV
    return [
        pl.BlockSpec((LEN, DK), lambda s, h: (s, h)),
        pl.BlockSpec((LEN, DK), lambda s, h: (s, heads_n + h)),
        pl.BlockSpec((LEN, DV), lambda s, h: (s, col_v + h)),
        pl.BlockSpec((LEN, DV), lambda s, h: (s, col_v + heads_n + h)),
        pl.BlockSpec((LEN, 128), lambda s, h: (s, 2 * heads_n + 4 * heads_n)),
        pl.BlockSpec((4, DK), lambda s, h: (0, h)),
        pl.BlockSpec((4, DK), lambda s, h: (0, h)),
        pl.BlockSpec((4, DV), lambda s, h: (0, h)),
        pl.BlockSpec((8, 128), lambda s, h: (0, 0)),
        pl.BlockSpec((1, DV), lambda s, h: (0, 0)),
    ]


def saved_specs(heads_n):
    return [
        pl.BlockSpec((LEN, DV), lambda s, h: (s, h)),
        pl.BlockSpec((LEN, DV), lambda s, h: (s, h)),
        pl.BlockSpec((1, 1, PARTS, CHUNK, CHUNK), lambda s, h: (s, h, 0, 0, 0)),
        pl.BlockSpec((1, 1, PARTS, DK, DV), lambda s, h: (s, h, 0, 0, 0)),
    ]


def mix_forward(proj, cq, ck, cv, heads_in, gain):
    rows = proj.shape[0]
    seqs, heads_n = rows // LEN, cq.shape[1] // DK
    wide = jax.ShapeDtypeStruct((rows, heads_n * DV), BF16)
    return pl.pallas_call(
        functools.partial(forward_kernel, heads_n),
        grid=(seqs, heads_n),
        in_specs=specs(heads_n),
        out_specs=[pl.BlockSpec((LEN, DV), lambda s, h: (s, h))] + saved_specs(heads_n),
        out_shape=[
            wide, wide, wide,
            jax.ShapeDtypeStruct((seqs, heads_n, PARTS, CHUNK, CHUNK), BF16),
            jax.ShapeDtypeStruct((seqs, heads_n, PARTS, DK, DV), BF16),
        ],
        cost_estimate=pl.CostEstimate(flops=2 * 10**9, bytes_accessed=25 * 10**6, transcendentals=10**6),
        name="mix_forward",
    )(proj, proj, proj, proj, proj, cq, ck, cv, heads_in, gain)


def mix_backward(proj, cq, ck, cv, heads_in, gain, grad, saved):
    rows, cols = proj.shape
    seqs, heads_n = rows // LEN, cq.shape[1] // DK
    return pl.pallas_call(
        functools.partial(backward_kernel, heads_n),
        grid=(seqs, heads_n),
        in_specs=specs(heads_n) + [pl.BlockSpec((LEN, DV), lambda s, h: (s, h))] + saved_specs(heads_n),
        out_specs=[
            pl.BlockSpec((LEN, cols), lambda s, h: (s, 0)),
            pl.BlockSpec((1, 1, 16, DV), lambda s, h: (s, h, 0, 0)),
        ],
        out_shape=[
            jax.ShapeDtypeStruct((rows, cols), BF16),
            jax.ShapeDtypeStruct((seqs, heads_n, 16, DV), F32),
        ],
        scratch_shapes=[pltpu.VMEM((LEN, 128), F32)],
        cost_estimate=pl.CostEstimate(flops=5 * 10**9, bytes_accessed=40 * 10**6, transcendentals=10**6),
        name="mix_backward",
    )(proj, proj, proj, proj, proj, cq, ck, cv, heads_in, gain, grad, *saved)


def matmul(left, right):
    return jnp.dot(left, right, preferred_element_type=F32)


def rows_inner(left, right):
    return lax.dot_general(left, right, (((0,), (0,)), ((), ())), preferred_element_type=F32)


def against_rows(left, right):
    return lax.dot_general(left, right, (((1,), (1,)), ((), ())), preferred_element_type=F32)


def row_factor(values):
    return lax.rsqrt(jnp.mean(values * values, axis=-1, keepdims=True) + 1e-05)


def norm_backward(values, factor, gain, grad):
    normed = values * factor
    inner = grad * gain
    spread = jnp.mean(inner * normed, axis=-1, keepdims=True)
    return factor * (inner - normed * spread), jnp.sum(grad * normed, axis=0)


SWAP = [(0, 1), (1, 0)]


def swap(value, axis):
    return lax.ppermute(value, axis, SWAP)


def gather_rows(shard):
    mine = lax.all_gather(shard, "chip", axis=0, tiled=True)
    other = swap(mine, "core")
    first = lax.axis_index("core") == 0
    count = shard.shape[0]
    even = jnp.where(first, mine, other).reshape(-1, 1, count, shard.shape[1])
    odd = jnp.where(first, other, mine).reshape(-1, 1, count, shard.shape[1])
    return jnp.concatenate([even, odd], axis=1).reshape(-1, shard.shape[1])


def core_columns(values, chips):
    core = lax.axis_index("core")
    split = values.reshape(values.shape[0], chips, 2, -1)
    mine = lax.dynamic_index_in_dim(split, core, 2, keepdims=False)
    other = lax.dynamic_index_in_dim(split, 1 - core, 2, keepdims=False)
    return mine.reshape(values.shape[0], -1), other.reshape(values.shape[0], -1)


def weight_grad(columns, grads):
    mine, other = columns
    sent = jnp.concatenate([rows_inner(other, grad).astype(BF16) for grad in grads], axis=1)
    came = swap(sent, "core")
    kept, at = [], 0
    for grad in grads:
        kept.append((rows_inner(mine, grad) + came[:, at : at + grad.shape[1]].astype(F32)).astype(BF16))
        at += grad.shape[1]
    return jnp.concatenate(kept, axis=1)


def all_sum(value, axis, size):
    step = 1
    while step < size:
        value = value + lax.ppermute(value, axis, [(at, at ^ step) for at in range(size)])
        step *= 2
    return value


def local(chips, tokens, norm_gain1, w_query, w_key, w_value, w_gate, w_decay, w_write, conv_query, conv_key,
          conv_value, a_log, dt_bias, out_gain, w_out, norm_gain2, w_ffgate, w_ffup, w_ffdown, cotangent):
    heads_n = a_log.shape[0]
    half = tokens.shape[0]
    pad = jnp.zeros((w_query.shape[0], 128 - 2 * heads_n), BF16)
    mix_shard = jnp.concatenate([w_query, w_key, w_value, w_gate, w_decay, w_write, pad], axis=1)
    late_shard = jnp.concatenate([w_out.T, w_ffgate, w_ffup, w_ffdown.T], axis=1)
    ff = w_ffgate.shape[1]
    wide = w_out.shape[0]
    tokens_other = swap(tokens, "tensor")
    cot = jnp.concatenate([cotangent, swap(cotangent, "tensor")], axis=0)
    w_mix = gather_rows(mix_shard)
    w_late = gather_rows(late_shard)
    w_out_t, w_gu, w_down_t = w_late[:, :wide], w_late[:, wide : wide + 2 * ff], w_late[:, wide + 2 * ff :]

    tokens32 = jnp.concatenate([tokens, tokens_other], axis=0).astype(F32)
    factor1 = row_factor(tokens32)
    normed1 = (tokens32 * factor1 * norm_gain1).astype(BF16)
    proj = matmul(normed1, w_mix)
    heads_in = jnp.pad(jnp.stack([a_log, dt_bias]), ((0, 6), (0, 128 - heads_n)))
    gain = out_gain.reshape(1, -1)
    gated, *saved = mix_forward(proj, conv_query, conv_key, conv_value, heads_in, gain)
    mix_part = against_rows(gated, w_out_t)
    resid1 = tokens32[:half] + mix_part[:half] + swap(mix_part[half:].astype(BF16), "tensor").astype(F32)
    factor2 = row_factor(resid1)
    normed2_own = (resid1 * factor2 * norm_gain2).astype(BF16)
    normed2 = jnp.concatenate([normed2_own, swap(normed2_own, "tensor")], axis=0)

    gate_up = matmul(normed2, w_gu)
    gate_val, up_val = gate_up[:, :ff], gate_up[:, ff:]
    gate_sig = jax.nn.sigmoid(gate_val)
    act = gate_val * gate_sig
    hidden = (act * up_val).astype(BF16)
    ffn_part = against_rows(hidden, w_down_t)
    result = resid1 + ffn_part[:half] + swap(ffn_part[half:].astype(BF16), "tensor").astype(F32)

    grad_hidden = matmul(cot, w_down_t)
    grad_gate = (grad_hidden * up_val * (gate_sig + act * (1.0 - gate_sig))).astype(BF16)
    grad_up = (grad_hidden * act).astype(BF16)
    grad_normed2 = against_rows(grad_gate, w_gu[:, :ff]) + against_rows(grad_up, w_gu[:, ff:])
    grad_rows2 = grad_normed2[:half] + swap(grad_normed2[half:].astype(BF16), "tensor").astype(F32)
    grad_norm, grad_gain2 = norm_backward(resid1, factor2, norm_gain2, grad_rows2)
    grad_resid = cotangent.astype(F32) + grad_norm
    resid_own = grad_resid.astype(BF16)
    resid_full = jnp.concatenate([resid_own, swap(resid_own, "tensor")], axis=0)
    grad_gated = matmul(resid_full, w_out_t)

    ffn_sum = jnp.concatenate(
        [weight_grad(core_columns(normed2, chips), (grad_gate, grad_up)), weight_grad(core_columns(cot, chips), (hidden,)),
         weight_grad(core_columns(resid_full, chips), (gated,))], axis=1)
    ffn_sum = lax.psum_scatter(ffn_sum, "chip", scatter_dimension=0, tiled=True).astype(F32)

    grad_proj, small = mix_backward(proj, conv_query, conv_key, conv_value, heads_in, gain, grad_gated, saved)
    small = jnp.sum(small, axis=0)
    small = all_sum(all_sum(small.reshape(-1, DV), "core", 2), "chip", chips).reshape(heads_n, 16, DV)
    mix_sum = weight_grad(core_columns(normed1, chips), (grad_proj,))
    mix_sum = lax.psum_scatter(mix_sum, "chip", scatter_dimension=0, tiled=True).astype(F32)
    grad_normed1 = against_rows(grad_proj, w_mix)
    grad_rows1 = grad_normed1[:half] + swap(grad_normed1[half:].astype(BF16), "tensor").astype(F32)
    grad_norm1, grad_gain1 = norm_backward(tokens32[:half], factor1[:half], norm_gain1, grad_rows1)
    grad_tokens = grad_resid + grad_norm1
    gain_rows = jnp.concatenate([grad_gain1.reshape(-1, 128), grad_gain2.reshape(-1, 128)], axis=0)
    gain_rows = all_sum(all_sum(all_sum(gain_rows, "core", 2), "tensor", 2), "chip", chips)
    out_gain_sum = all_sum(jnp.sum(small[:, 8], axis=0, keepdims=True), "tensor", 2)

    key_w, val_w = heads_n * DK, heads_n * DV

    def taps(rows):
        return jnp.transpose(rows, (1, 0, 2)).reshape(4, -1)

    decay_at = 2 * key_w + 2 * val_w
    return (
        result.astype(BF16),
        grad_tokens,
        gain_rows[: gain_rows.shape[0] // 2].reshape(-1),
        mix_sum[:, :key_w],
        mix_sum[:, key_w : 2 * key_w],
        mix_sum[:, 2 * key_w : 2 * key_w + val_w],
        mix_sum[:, 2 * key_w + val_w : decay_at],
        mix_sum[:, decay_at : decay_at + heads_n],
        mix_sum[:, decay_at + heads_n : decay_at + 2 * heads_n],
        taps(small[:, 4:8, :DK]),
        taps(small[:, 4:8, DK:]),
        taps(small[:, :4]),
        small[:, 9, 0],
        small[:, 9, 1],
        out_gain_sum.reshape(-1),
        ffn_sum[:, 3 * ff :].T,
        gain_rows[gain_rows.shape[0] // 2 :].reshape(-1),
        ffn_sum[:, :ff],
        ffn_sum[:, ff : 2 * ff],
        ffn_sum[:, 2 * ff : 3 * ff].T,
    )


def solution(mesh):
    chips = mesh.shape["dp"] // 2
    inner = jax.sharding.Mesh(mesh.devices.reshape(chips, 2, -1), ("chip", "core", "tensor"))
    dp, rows, every = ("chip", "core"), P(("chip", "core", "tensor"), None), P()
    down, across, taps, head = P(dp, "tensor"), P("tensor", dp), P(None, "tensor"), P("tensor")
    return jax.shard_map(
        functools.partial(local, chips),
        mesh=inner,
        in_specs=(rows, every, down, down, down, down, down, down, taps, taps, taps, head, head, every, across, every,
                  down, down, across, rows),
        out_specs=(rows, rows, every, down, down, down, down, down, down, taps, taps, taps, head, head, every, across,
                   every, down, down, across),
        check_vma=False,
    )
```

```python
import functools
import math

import jax
import jax.numpy as jnp
from jax import lax
from jax.experimental import pallas as pl
from jax.experimental.pallas import tpu as pltpu
from jax.sharding import PartitionSpec as P


F32 = jnp.float32
BF16 = jnp.bfloat16
LEN = 512
DK = 128
DV = 256
CHUNK = 128
FF_HALF = 768
PARTS = LEN // CHUNK


def dot_nn(a, b):
    return lax.dot_general(a, b, (((1,), (0,)), ((), ())), preferred_element_type=F32)


def dot_nt(a, b):
    return lax.dot_general(a, b, (((1,), (1,)), ((), ())), preferred_element_type=F32)


def dot_tn(a, b):
    return lax.dot_general(a, b, (((0,), (0,)), ((), ())), preferred_element_type=F32)


def sigmoid(x):
    return 1.0 / (1.0 + jnp.exp(-x))


def softplus(x):
    return jnp.maximum(x, 0.0) + jnp.log1p(jnp.exp(-jnp.abs(x)))


def exact_rows(rows, ones):
    first = rows.astype(BF16)
    rest = rows - first.astype(F32)
    second = rest.astype(BF16)
    third = (rest - second.astype(F32)).astype(BF16)
    return dot_nn(first, ones) + dot_nn(second, ones) + dot_nn(third, ones)


def iota2(rows, cols, axis):
    return lax.broadcasted_iota(jnp.int32, (rows, cols), axis)


def same_group(size):
    shift = size.bit_length() - 1
    return (iota2(CHUNK, CHUNK, 0) >> shift) == (iota2(CHUNK, CHUNK, 1) >> shift)


def tri(upper):
    row, col = iota2(CHUNK, CHUNK, 0), iota2(CHUNK, CHUNK, 1)
    keep = row <= col if upper else row >= col
    return keep.astype(F32).astype(BF16)


def spread(row):
    return jnp.broadcast_to(row, (CHUNK, CHUNK)).T


def twice(x):
    return jnp.concatenate([x, x], axis=1)


def odd_blocks(x, size):
    return jnp.concatenate([x[at : at + size] for at in range(size, CHUNK, 2 * size)], axis=0)


def weave(even, odd, size):
    parts = []
    for at in range(0, CHUNK // 2, size):
        parts += [even[at : at + size], odd[at : at + size]]
    return jnp.concatenate(parts, axis=0)


def invert_all(lowers):
    in8 = same_group(8)
    lane = iota2(8, CHUNK, 1) & 7
    place = iota2(8, CHUNK, 0)
    small = [jnp.sum(jnp.where(in8, lower, 0.0).reshape(CHUNK // 8, 8, CHUNK), axis=0) for lower in lowers]
    masked = [jnp.where(lane == at, member, 0.0) for member in small for at in range(7)]
    columns = dot_nn(jnp.concatenate(masked, axis=0).astype(BF16), in8.astype(F32).astype(BF16))
    inverse = []
    for which in range(len(lowers)):
        solved = jnp.where(lane == place, 1.0, 0.0)
        for at in range(7):
            start = (which * 7 + at) * 8
            solved = solved - columns[start : start + 8] * jnp.broadcast_to(solved[at : at + 1], (8, CHUNK))
        inverse.append(jnp.where(in8, jnp.concatenate([solved] * (CHUNK // 8), axis=0), 0.0))
    size = 8
    while size < CHUNK:
        ring = jnp.logical_and(same_group(2 * size), jnp.logical_not(same_group(size)))
        between = [odd_blocks(jnp.where(ring, lower, 0.0), size).astype(BF16) for lower in lowers]
        low = [member.astype(BF16) for member in inverse]
        inner = [dot_nn(a, b) for a, b in zip(between, low)]
        padded = [weave(jnp.zeros_like(member), member, size).astype(BF16) for member in inner]
        odd = [odd_blocks(member, size) for member in inverse]
        new_odd = [a - dot_nn(a.astype(BF16), b) for a, b in zip(odd, padded)]
        even = [
            jnp.concatenate([member[at : at + size] for at in range(0, CHUNK, 2 * size)], axis=0) for member in inverse
        ]
        inverse = [weave(a, b, size) for a, b in zip(even, new_odd)]
        size *= 2
    return [member.astype(BF16) for member in inverse]


def head_value(heads_ref, row, head):
    values = heads_ref[row : row + 1, :]
    lane = lax.broadcasted_iota(jnp.int32, values.shape, 1)
    return jnp.sum(jnp.where(lane == head, values, 0.0), axis=1, keepdims=True)


def head_rates(ab_ref, heads_ref, head, heads_n):
    decay_in = ab_ref[pl.ds(head, 1), :] + head_value(heads_ref, 1, head)
    write = sigmoid(ab_ref[pl.ds(heads_n + head, 1), :])
    rate = -jnp.exp(head_value(heads_ref, 0, head))
    soft = softplus(decay_in)
    decay = rate * soft
    rows = [decay[:, at * CHUNK : (at + 1) * CHUNK] for at in range(PARTS)]
    stacked = jnp.concatenate(rows + [jnp.zeros((8 - PARTS, CHUNK), F32)], axis=0)
    return write, decay_in, rate, soft, exact_rows(stacked, tri(True))


def convolve(ref, part, taps):
    body = ref[pl.ds(part * CHUNK, CHUNK), :]
    if part == 0:
        head = jnp.zeros((8, body.shape[1]), F32)
    else:
        head = ref[pl.ds(part * CHUNK - 8, 8), :]
    rows = jnp.concatenate([head, body], axis=0)
    total = body * taps[3:4, :]
    for tap in range(3):
        total = total + rows[5 + tap : 5 + tap + CHUNK, :] * taps[tap : tap + 1, :]
    return total


def chunk_core(xq, xk, xv, write_row, total_row):
    row, col = iota2(CHUNK, CHUNK, 0), iota2(CHUNK, CHUNK, 1)
    gq, gk, gv = sigmoid(xq), sigmoid(xk), sigmoid(xv)
    sq, sk, values = xq * gq, xk * gk, xv * gv
    rq = lax.rsqrt(jnp.sum(sq * sq, axis=1, keepdims=True) + 1e-06)
    rk = lax.rsqrt(jnp.sum(sk * sk, axis=1, keepdims=True) + 1e-06)
    queries = sq * (rq * (1.0 / math.sqrt(DK)))
    keys = sk * rk
    q_low, k_low = queries.astype(BF16), keys.astype(BF16)
    write, total = spread(write_row), spread(total_row)
    fade = jnp.where(row >= col, jnp.exp(jnp.minimum(total - total_row, 0.0)), 0.0)
    fade_strict = jnp.where(row > col, fade, 0.0)
    key_inner = dot_nt(k_low, k_low)
    last_row = total_row[:, CHUNK - 1 : CHUNK]
    from_start = jnp.exp(total)
    to_end = jnp.exp(last_row - total)
    return dict(
        gq=gq, gk=gk, gv=gv, rq=rq, rk=rk, queries=queries, keys=keys, values=values, q_low=q_low, k_low=k_low,
        write=write, fade=fade, fade_strict=fade_strict, key_inner=key_inner, scores=dot_nt(q_low, k_low) * fade,
        lower=write * key_inner * fade_strict, from_start=from_start, to_end=to_end, last=jnp.exp(last_row),
        key_start=(write * from_start) * keys, q_start=queries * from_start, key_end=keys * to_end,
    )


def forward_kernel(heads_n, x_ref, wq_ref, wk_ref, wv_ref, wg_ref, wab_ref, cq_ref, ck_ref, cv_ref, heads_ref,
                   gain_ref, gated_ref, mixed_ref, delta_ref, solve_ref, state_ref, pq_ref, pk_ref, pv_ref, pg_ref,
                   xq_ref, xk_ref, xv_ref, ab_ref, turned):
    head = pl.program_id(0)

    @pl.when(head == 0)
    def _():
        turned[...] = dot_nn(x_ref[...], wab_ref[...]).T
        ab_ref[...] = turned[0:8, :]

    pq_ref[...] = dot_nn(x_ref[...], wq_ref[...])
    pk_ref[...] = dot_nn(x_ref[...], wk_ref[...])
    pv_ref[...] = dot_nn(x_ref[...], wv_ref[...])
    pg_ref[...] = dot_nn(x_ref[...], wg_ref[...])
    gain = gain_ref[0:1, :]
    write, _, _, _, totals = head_rates(turned, heads_ref, head, heads_n)
    cores = []
    for part in range(PARTS):
        span = pl.ds(part * CHUNK, CHUNK)
        xs = [convolve(ref, part, taps[...]) for ref, taps in ((pq_ref, cq_ref), (pk_ref, ck_ref), (pv_ref, cv_ref))]
        for ref, value in zip((xq_ref, xk_ref, xv_ref), xs):
            ref[span, :] = value
        cores.append(chunk_core(*xs, write[:, part * CHUNK : (part + 1) * CHUNK], totals[part : part + 1, :]))
    solves = invert_all([core["lower"] for core in cores])
    for part in range(PARTS):
        solve_ref[0, 0, part] = solves[part]
    value_parts = [dot_nn(t, (twice(c["write"]) * c["values"]).astype(BF16)) for t, c in zip(solves, cores)]
    key_parts = [dot_nn(t, c["key_start"].astype(BF16)).astype(BF16) for t, c in zip(solves, cores)]
    state = jnp.zeros((DK, DV), F32)
    for part in range(PARTS):
        core = cores[part]
        state_low = state.astype(BF16)
        state_ref[0, 0, part] = state_low
        update = value_parts[part] - dot_nn(key_parts[part], state_low)
        update_low = update.astype(BF16)
        mixed = dot_nn(core["q_start"].astype(BF16), state_low) + dot_nn(core["scores"].astype(BF16), update_low)
        if part < PARTS - 1:
            state = core["last"] * state + dot_tn(core["key_end"].astype(BF16), update_low)
        span = pl.ds(part * CHUNK, CHUNK)
        delta_ref[span, :] = update_low
        mixed_ref[span, :] = mixed.astype(BF16)
        factor = lax.rsqrt(jnp.mean(mixed * mixed, axis=1, keepdims=True) + 1e-05)
        gate_in = pg_ref[span, :]
        gated_ref[span, :] = (mixed * factor * gain * (gate_in * sigmoid(gate_in))).astype(BF16)


def backward_kernel(heads_n, resid_ref, wo_ref, cq_ref, ck_ref, cv_ref, heads_ref, gain_ref, mixed_ref, delta_ref,
                    solve_ref, state_ref, pq_ref, pk_ref, pv_ref, pg_ref, xq_ref, xk_ref, xv_ref, ab_ref, *refs):
    dp_ref, small_ref, grad_ref, turned = refs[-4:]
    head = pl.program_id(0)
    row, col = iota2(CHUNK, CHUNK, 0), iota2(CHUNK, CHUNK, 1)
    gain = gain_ref[0:1, :]
    width_k, width_v = heads_n * DK, heads_n * DV
    scale = 1.0 / math.sqrt(DK)

    def fold(x):
        return jnp.sum(x.reshape(CHUNK // 8, 8, x.shape[1]), axis=0)

    def down(x):
        return jnp.sum(x, axis=0, keepdims=True)

    @pl.when(head == 0)
    def _():
        turned[...] = jnp.zeros_like(turned)

    grad_ref[...] = dot_nn(resid_ref[...], wo_ref[...])
    write_row, decay_in, rate, soft, totals = head_rates(ab_ref, heads_ref, head, heads_n)
    state_grad = jnp.zeros((DK, DV), F32)
    gain_sum = jnp.zeros((8, DV), F32)
    taps_sum = {name: [jnp.zeros((8, size), F32) for _ in range(4)] for name, size in (("q", DK), ("k", DK), ("v", DV))}
    following = {"q": jnp.zeros((8, DK), F32), "k": jnp.zeros((8, DK), F32), "v": jnp.zeros((8, DV), F32)}
    rate_sum = jnp.zeros((1, CHUNK), F32)
    bias_sum = jnp.zeros((1, CHUNK), F32)
    suffix, which = tri(False), iota2(8, CHUNK, 0)
    for part in reversed(range(PARTS)):
        span = pl.ds(part * CHUNK, CHUNK)
        piece = slice(part * CHUNK, (part + 1) * CHUNK)
        xq, xk, xv = xq_ref[span, :], xk_ref[span, :], xv_ref[span, :]
        core = chunk_core(xq, xk, xv, write_row[:, piece], totals[part : part + 1, :])
        write, keys, queries, values = core["write"], core["keys"], core["queries"], core["values"]
        k_low, q_low, fade = core["k_low"], core["q_low"], core["fade"]
        solve, state_low, delta = solve_ref[0, 0, part], state_ref[0, 0, part], delta_ref[span, :]
        mixed = mixed_ref[span, :].astype(F32)
        factor = lax.rsqrt(jnp.mean(mixed * mixed, axis=1, keepdims=True) + 1e-05)
        normed = mixed * factor
        gate_in = pg_ref[span, :]
        gate_sig = sigmoid(gate_in)
        gate = gate_in * gate_sig
        grad = grad_ref[span, :]
        plain = grad * normed
        gain_sum = gain_sum + fold(plain * gate)
        dp_ref[span, pl.ds(pl.multiple_of(2 * width_k + width_v + head * DV, DV), DV)] = (
            plain * gain * (gate_sig + gate * (1.0 - gate_sig))
        ).astype(BF16)
        normed_grad = grad * gate * gain
        mixed_grad = factor * (normed_grad - normed * jnp.mean(normed_grad * normed, axis=1, keepdims=True))
        mixed_low = mixed_grad.astype(BF16)
        key_part = dot_nn(solve, core["key_start"].astype(BF16)).astype(BF16)
        grad_low = state_grad.astype(BF16)
        update_grad = dot_tn(core["scores"].astype(BF16), mixed_low) + dot_nn(core["key_end"].astype(BF16), grad_low)
        update_low = update_grad.astype(BF16)
        key_end_grad = dot_nt(delta, grad_low)
        last_grad = jnp.sum(state_low.astype(F32) * state_grad)
        if part > 0:
            state_grad = (
                core["last"] * state_grad
                + dot_tn(core["q_start"].astype(BF16), mixed_low)
                - dot_tn(key_part, update_low)
            )
        q_start_grad = dot_nt(mixed_low, state_low)
        scores_grad = dot_nt(mixed_low, delta)
        right_grad = dot_tn(solve, update_low)
        right_low = right_grad.astype(BF16)
        lower_grad = jnp.where(row > col, -dot_nt(right_low, delta), 0.0)
        key_start_grad = -dot_nt(right_low, state_low)
        inner_low = (scores_grad * fade).astype(BF16)
        queries_grad = q_start_grad * core["from_start"] + dot_nn(inner_low, k_low)
        faded_lower = lower_grad * core["fade_strict"]
        key_inner_grad = write * faded_lower
        both = (key_inner_grad + key_inner_grad.T).astype(BF16)
        keys_grad = (
            key_end_grad * core["to_end"]
            + key_start_grad * (write * core["from_start"])
            + dot_tn(inner_low, q_low)
            + dot_nn(both, k_low)
        )
        values_grad = twice(write) * right_grad
        start_keys = key_start_grad * core["from_start"] * keys
        value_terms = right_grad * values
        write_grad = down(
            (start_keys + faded_lower * core["key_inner"] + value_terms[:, :CHUNK] + value_terms[:, CHUNK:]).T
        )
        ends = key_end_grad * core["key_end"]
        gaps_grad = scores_grad * core["scores"] + lower_grad * core["lower"]
        total_grad = down((q_start_grad * core["q_start"] + write * start_keys - ends + gaps_grad).T) - down(gaps_grad)
        at_end = jnp.sum(ends) + last_grad * core["last"]
        decay_grad = exact_rows(jnp.broadcast_to(total_grad, (8, CHUNK)), suffix)[0:1, :] + at_end
        rate_sum = rate_sum + decay_grad * (rate * soft[:, piece])
        decay_in_grad = decay_grad * (rate * sigmoid(decay_in[:, piece]))
        bias_sum = bias_sum + decay_in_grad
        write_in_grad = write_grad * (write_row[:, piece] * (1.0 - write_row[:, piece]))
        held = jnp.where(which == head, decay_in_grad, turned[0:8, span])
        turned[0:8, span] = jnp.where(which == heads_n + head, write_in_grad, held)
        unit = queries * (1.0 / scale)
        sq_grad = (core["rq"] * scale) * (
            queries_grad - unit * jnp.sum(queries_grad * unit, axis=1, keepdims=True)
        )
        sk_grad = core["rk"] * (keys_grad - keys * jnp.sum(keys_grad * keys, axis=1, keepdims=True))
        for name, grad_in, x, sig, p_ref, taps_ref, start, size in (
            ("q", sq_grad, xq, core["gq"], pq_ref, cq_ref, 0, DK),
            ("k", sk_grad, xk, core["gk"], pk_ref, ck_ref, width_k, DK),
            ("v", values_grad, xv, core["gv"], pv_ref, cv_ref, 2 * width_k, DV),
        ):
            taps, rows = taps_ref[...], p_ref[span, :]
            x_grad = grad_in * (sig + x * sig * (1.0 - sig))
            longer = jnp.concatenate([x_grad, following[name]], axis=0)
            following[name] = x_grad[0:8, :]
            taps_sum[name][3] = taps_sum[name][3] + fold(rows * x_grad)
            proj = x_grad * taps[3:4, :]
            for tap in range(3):
                moved = longer[3 - tap : 3 - tap + CHUNK, :]
                taps_sum[name][tap] = taps_sum[name][tap] + fold(rows * moved)
                proj = proj + moved * taps[tap : tap + 1, :]
            dp_ref[span, pl.ds(pl.multiple_of(start + head * size, size), size)] = proj.astype(BF16)

    @pl.when(head == heads_n - 1)
    def _():
        dp_ref[:, pl.ds(2 * width_k + 2 * width_v, 128)] = turned[...].T.astype(BF16)

    lane = iota2(1, DV, 1)
    rates, biases = jnp.sum(rate_sum, axis=1, keepdims=True), jnp.sum(bias_sum, axis=1, keepdims=True)
    small = [down(taps_sum["v"][tap]) for tap in range(4)]
    small += [jnp.concatenate([down(taps_sum["q"][tap]), down(taps_sum["k"][tap])], axis=1) for tap in range(4)]
    small += [down(gain_sum), jnp.where(lane == 0, rates, 0.0) + jnp.where(lane == 1, biases, 0.0)]
    small += [jnp.zeros((6, DV), F32)]
    small_ref[0, 0] = jnp.concatenate(small, axis=0)


def param_specs():
    return [
        pl.BlockSpec((4, DK), lambda h: (0, h)),
        pl.BlockSpec((4, DK), lambda h: (0, h)),
        pl.BlockSpec((4, DV), lambda h: (0, h)),
        pl.BlockSpec((8, 128), lambda h: (0, 0)),
        pl.BlockSpec((1, DV), lambda h: (0, 0)),
    ]


def saved_specs():
    narrow, wide = pl.BlockSpec((LEN, DK), lambda h: (0, h)), pl.BlockSpec((LEN, DV), lambda h: (0, h))
    return [
        wide, wide,
        pl.BlockSpec((1, 1, PARTS, CHUNK, CHUNK), lambda h: (0, h, 0, 0, 0)),
        pl.BlockSpec((1, 1, PARTS, DK, DV), lambda h: (0, h, 0, 0, 0)),
        narrow, narrow, wide, wide, narrow, narrow, wide,
        pl.BlockSpec((8, LEN), lambda h: (0, 0)),
    ]


def mix_forward(normed, weights, seq, params):
    width, heads_n = normed.shape[1], params[0].shape[1] // DK
    col_q, col_v = heads_n * DV // DK, heads_n + 2 * heads_n * DK // DV

    def shape(*dims, kind=F32):
        return jax.ShapeDtypeStruct(dims, kind)

    low = shape(LEN, heads_n * DV, kind=BF16)
    narrow, wide = shape(LEN, heads_n * DK), shape(LEN, heads_n * DV)
    return pl.pallas_call(
        functools.partial(forward_kernel, heads_n),
        grid=(heads_n,),
        in_specs=[
            pl.BlockSpec((LEN, width), lambda h: (seq, 0)),
            pl.BlockSpec((width, DK), lambda h: (0, col_q + h)),
            pl.BlockSpec((width, DK), lambda h: (0, col_q + heads_n + h)),
            pl.BlockSpec((width, DV), lambda h: (0, col_v + h)),
            pl.BlockSpec((width, DV), lambda h: (0, col_v + heads_n + h)),
            pl.BlockSpec((width, 128), lambda h: (0, col_q + 6 * heads_n)),
        ] + param_specs(),
        out_specs=[pl.BlockSpec((LEN, DV), lambda h: (0, h))] + saved_specs(),
        out_shape=[
            low, low, low,
            shape(1, heads_n, PARTS, CHUNK, CHUNK, kind=BF16),
            shape(1, heads_n, PARTS, DK, DV, kind=BF16),
            narrow, narrow, wide, wide, narrow, narrow, wide,
            shape(8, LEN),
        ],
        scratch_shapes=[pltpu.VMEM((128, LEN), F32)],
        cost_estimate=pl.CostEstimate(flops=3 * 10**9 * heads_n, bytes_accessed=5 * 10**6 * heads_n, transcendentals=10**6),
        name="mix_forward",
    )(normed, *[weights] * 5, *params)


def mix_backward(resid, w_out, seq, params, saved, cols, earlier=None):
    heads_n, width = params[0].shape[1] // DK, resid.shape[1]
    held = [earlier] if earlier is not None else []
    return pl.pallas_call(
        functools.partial(backward_kernel, heads_n),
        grid=(heads_n,),
        in_specs=[pl.BlockSpec((LEN, width), lambda h: (0, 0)), pl.BlockSpec((width, DV), lambda h: (0, h))]
        + param_specs() + saved_specs() + [pl.BlockSpec(memory_space=pl.ANY)] * len(held),
        out_specs=[
            pl.BlockSpec((LEN, cols), lambda h: (seq, 0)),
            pl.BlockSpec((1, 1, 16, DV), lambda h: (0, h, 0, 0)),
        ],
        out_shape=[
            jax.ShapeDtypeStruct((2 * LEN, cols), BF16),
            jax.ShapeDtypeStruct((1, heads_n, 16, DV), F32),
        ],
        scratch_shapes=[pltpu.VMEM((LEN, DV), F32), pltpu.VMEM((128, LEN), F32)],
        input_output_aliases={19: 0} if held else {},
        cost_estimate=pl.CostEstimate(flops=5 * 10**9 * heads_n, bytes_accessed=6 * 10**6 * heads_n, transcendentals=10**6),
        name="mix_backward",
    )(resid, w_out, *params, *saved, *held)


def ffn_kernel(held, x_ref, cot_ref, mine_ref, other_ref, *refs):
    outs, (w_ref, part_sum, back_sum, sems) = refs[held : held + 8], refs[held + 8 :]
    part_ref, back_ref = outs[6], outs[7]
    units = w_ref.shape[2]
    copies = []
    for half, source in enumerate((mine_ref, other_ref)):
        for at in range(3):
            slot = 3 * half + at
            copies.append(
                pltpu.make_async_copy(source.at[:, pl.ds(at * units, units)], w_ref.at[slot], sems.at[slot])
            )
    for copy in copies:
        copy.start()
    for half in range(2):
        at = 3 * half
        copies[at].wait()
        gate = dot_nn(x_ref[...], w_ref[at])
        copies[at + 1].wait()
        up = dot_nn(x_ref[...], w_ref[at + 1])
        copies[at + 2].wait()
        grad = dot_nn(cot_ref[...], w_ref[at + 2])
        sig = sigmoid(gate)
        act = gate * sig
        outs[at][...] = (act * up).astype(BF16)
        outs[at + 1][...] = (grad * up * (sig + act * (1.0 - sig))).astype(BF16)
        outs[at + 2][...] = (grad * act).astype(BF16)
        part = dot_nt(outs[at][...], w_ref[at + 2])
        back = dot_nt(outs[at + 1][...], w_ref[at]) + dot_nt(outs[at + 2][...], w_ref[at + 1])
        if half == 0:
            part_sum[...] = part
            back_sum[...] = back
        else:
            part_ref[...] = (part_sum[...] + part).astype(part_ref.dtype)
            back_ref[...] = (back_sum[...] + back).astype(back_ref.dtype)


def ffn_both(x, cot, mine, other, seq, total, kind, earlier=None):
    rows, width = x.shape
    units = FF_HALF
    whole = pl.BlockSpec((rows, width), lambda i: (0, 0))
    anywhere = pl.BlockSpec(memory_space=pl.ANY)
    tiles = pl.BlockSpec((rows, units), lambda i: (seq, 0))
    held = list(earlier) if earlier else []
    return pl.pallas_call(
        functools.partial(ffn_kernel, len(held)),
        grid=(1,),
        in_specs=[whole, whole, anywhere, anywhere] + [anywhere] * len(held),
        out_specs=[tiles] * 6 + [whole, whole],
        out_shape=[jax.ShapeDtypeStruct((total, units), BF16)] * 6 + [jax.ShapeDtypeStruct((rows, width), kind)] * 2,
        input_output_aliases={4 + at: at for at in range(len(held))},
        scratch_shapes=[pltpu.VMEM((6, width, units), BF16)] + [pltpu.VMEM((rows, width), F32)] * 2
        + [pltpu.SemaphoreType.DMA((6,))],
        cost_estimate=pl.CostEstimate(flops=24 * rows * width * units, bytes_accessed=25 * 10**6, transcendentals=rows * units * 2),
        name="ffn_both",
    )(x, cot, mine, other, *held)


def late_kernel(plan, held, *refs):
    lefts, rights = refs[: plan[0]], refs[plan[0] : plan[0] + len(plan[1])]
    out_ref, turned = refs[-2], refs[-1]
    step = pl.program_id(0)
    for at, (right, (source, fresh)) in enumerate(zip(rights, plan[1])):

        @pl.when(step == at)
        def _(right=right, source=source, fresh=fresh):
            if fresh:
                turned[:, :LEN] = lefts[2 * source][...].T
                turned[:, LEN:] = lefts[2 * source + 1][...].T
            total = dot_nn(turned[...], right[...])
            if held:
                total = total + refs[plan[0] + len(plan[1])][...].astype(F32)
            out_ref[...] = total.astype(BF16)


def late_grads(normed, cot, units, came=None):
    hidden, grad_gate, grad_up = units
    rows, tile = hidden.shape
    width = cot[0].shape[1]
    lefts, rights = [*normed, *cot], [grad_gate, grad_up, hidden]
    plan = (4, ((0, True), (0, False), (1, True)))
    across = pl.BlockSpec((width, tile), lambda i: (0, i))
    held = [came] if came is not None else []
    return pl.pallas_call(
        functools.partial(late_kernel, plan, len(held)),
        grid=(3,),
        in_specs=[pl.BlockSpec((LEN, width), lambda i: (0, 0))] * 4 + [pl.BlockSpec((rows, tile), lambda i: (0, 0))] * 3
        + [across] * len(held),
        out_specs=across,
        out_shape=jax.ShapeDtypeStruct((width, 3 * tile), BF16),
        scratch_shapes=[pltpu.VMEM((width, rows), BF16)],
        cost_estimate=pl.CostEstimate(flops=6 * rows * width * tile, bytes_accessed=16 * 10**6, transcendentals=0),
        name="late_grads",
    )(*lefts, *rights, *held)


def mix_kernel(held, resid_s, resid_o, normed_ref, gated_s, gated_o, grad_ref, *refs):
    out_ref, split = refs[-1], gated_s.shape[1]
    first = dot_nn(resid_s[...].T, gated_s[...]) + dot_nn(resid_o[...].T, gated_o[...])
    second = dot_nn(normed_ref[...].T, grad_ref[...])
    if held:
        first = first + refs[0][:, :split].astype(F32)
        second = second + refs[0][:, split:].astype(F32)
    out_ref[:, :split] = first.astype(BF16)
    out_ref[:, split:] = second.astype(BF16)


def mix_grads(resid, gated, normed, grads, came=None):
    (rows, width), tile = normed.shape, 256
    cols = gated[0].shape[1] + grads.shape[1]
    down = pl.BlockSpec((tile, cols), lambda i: (i, 0))
    held = [came] if came is not None else []
    whole = [pl.BlockSpec(value.shape, lambda i: (0, 0)) for value in (*gated, grads)]
    return pl.pallas_call(
        functools.partial(mix_kernel, len(held)),
        grid=(width // tile,),
        in_specs=[pl.BlockSpec((LEN, tile), lambda i: (0, i))] * 2 + [pl.BlockSpec((rows, tile), lambda i: (0, i))]
        + whole + [down] * len(held),
        out_specs=down,
        out_shape=jax.ShapeDtypeStruct((width, cols), BF16),
        cost_estimate=pl.CostEstimate(flops=2 * rows * width * cols, bytes_accessed=14 * 10**6, transcendentals=0),
        name="mix_grads",
    )(*resid, normed, *gated, grads, *held)


def back_kernel(skip, mine_ref, other_ref, w0_ref, w1_ref, unit_ref, out_ref, low_ref, gain_ref):
    total = dot_nt(mine_ref[...], w0_ref[:, skip:]) + dot_nt(other_ref[...], w1_ref[:, skip:])
    out_ref[...] = total
    low_ref[...] = total.astype(BF16)
    gain_ref[...] = jnp.sum(total * unit_ref[...], axis=0, keepdims=True)


def back_rows(grads, weights, unit, seq):
    (width, all_cols), cols, tile = weights[0].shape, grads[0].shape[1], 256
    rows = pl.BlockSpec((LEN, cols), lambda i: (seq, 0))
    rights = pl.BlockSpec((tile, all_cols), lambda i: (i, 0))
    outs = pl.BlockSpec((LEN, tile), lambda i: (0, i))
    return pl.pallas_call(
        functools.partial(back_kernel, all_cols - cols),
        grid=(width // tile,),
        in_specs=[rows, rows, rights, rights, pl.BlockSpec((LEN, tile), lambda i: (seq, i))],
        out_specs=[outs, outs, pl.BlockSpec((1, tile), lambda i: (0, i))],
        out_shape=[
            jax.ShapeDtypeStruct((LEN, width), F32),
            jax.ShapeDtypeStruct((LEN, width), BF16),
            jax.ShapeDtypeStruct((1, width), F32),
        ],
        cost_estimate=pl.CostEstimate(flops=4 * LEN * width * cols, bytes_accessed=17 * 10**6, transcendentals=0),
        name="back_rows",
    )(*grads, *weights, unit)


def against_rows(left, right):
    return lax.dot_general(left, right, (((1,), (1,)), ((), ())), preferred_element_type=F32)


def row_factor(values):
    return lax.rsqrt(jnp.mean(values * values, axis=-1, keepdims=True) + 1e-05)


def norm_backward(normed, factor, gain, grad):
    inner = grad * gain
    return factor * (inner - normed * jnp.mean(inner * normed, axis=-1, keepdims=True))


SWAP = [(0, 1), (1, 0)]


def swap(value, axis):
    return lax.ppermute(value, axis, SWAP)


def after(value, other):
    return lax.optimization_barrier((value, other))[0]


def by_core(mine, other):
    first = lax.axis_index("core") == 0
    return jnp.where(first, mine, other), jnp.where(first, other, mine)


def own_half(parts):
    return by_core(parts[0], parts[1])


def halves(value):
    size = value.shape[-1] // 2
    return value[..., :size], value[..., size:]


def chip_rows(parts):
    mine, other = own_half(parts)
    return jnp.concatenate(by_core(mine, swap(other, "core")), axis=0)


def wide_halves(value, size):
    return tuple(jnp.pad(part, ((0, 0), (0, size - part.shape[1]))) for part in halves(value))


class Ring:
    def __init__(self, chips):
        self.chips = chips
        order = list(range(0, chips, 2)) + list(range(chips - 1, 0, -2))
        after = order[1:] + order[:1]
        self.ahead, self.back = list(zip(order, after)), list(zip(after, order))
        me = lax.axis_index("chip")
        self.place = jnp.where(me % 2 == 0, me // 2, chips - 1 - me // 2)

    def chip_at(self, offset):
        place = (self.place + offset + self.chips) % self.chips
        return jnp.where(place < self.chips // 2, 2 * place, 2 * (self.chips - 1 - place) + 1)

    def gather(self, piece, joined):
        rows = piece.shape[0]
        pieces, offsets = [piece], [0]
        up = down = piece
        steps = (self.chips - 1) // 2
        for step in range(1, steps + 1):
            up, down = lax.ppermute(up, "chip", self.ahead), lax.ppermute(down, "chip", self.back)
            up, down = lax.optimization_barrier((up, down))
            pieces += [up, down]
            offsets += [-step, step]
        far = self.chips // 2
        top = lax.ppermute(up[: rows // 2], "chip", self.ahead)
        bottom = lax.ppermute(down[rows // 2 :], "chip", self.back)
        pieces += lax.optimization_barrier((top, bottom))
        return joined(pieces, [self.chip_at(offset) for offset in offsets + [far]])

    def by_slices(self, pieces, places):
        rows, cols = pieces[0].shape
        full = jnp.zeros((self.chips, rows, cols), pieces[0].dtype)
        starts = [0] * (len(pieces) - 1) + [rows // 2]
        for value, place, start in zip(pieces, places + places[-1:], starts):
            full = lax.dynamic_update_slice(full, value[None], (place, start, 0))
        return full.reshape(-1, cols)

    def by_copies(self, pieces, places):
        rows, cols = pieces[0].shape
        count = len(pieces)

        def kernel(places_ref, *refs):
            out_ref, held, into, out = refs[count:]
            firsts = [at * rows for at in range(count - 1)] + [(count - 2) * rows + rows // 2]
            stages, results = [], []
            for at, ref in enumerate(refs[:count]):
                start = pl.multiple_of(places_ref[min(at, count - 2)] * rows, rows)
                if at == count - 1:
                    start = pl.multiple_of(start + rows // 2, rows // 2)
                slot = held.at[pl.ds(firsts[at], ref.shape[0]), :]
                stages.append(pltpu.make_async_copy(ref, slot, into.at[at]))
                results.append(pltpu.make_async_copy(slot, out_ref.at[pl.ds(start, ref.shape[0]), :], out.at[at]))
                stages[-1].start()
            for stage, result in zip(stages, results):
                stage.wait()
                result.start()
            for result in results:
                result.wait()

        return pl.pallas_call(
            kernel,
            grid_spec=pltpu.PrefetchScalarGridSpec(
                num_scalar_prefetch=1,
                grid=(1,),
                in_specs=[pl.BlockSpec(memory_space=pl.ANY)] * count,
                out_specs=pl.BlockSpec(memory_space=pl.ANY),
                scratch_shapes=[pltpu.VMEM((self.chips * rows, cols), pieces[0].dtype)]
                + [pltpu.SemaphoreType.DMA((count,))] * 2,
            ),
            out_shape=jax.ShapeDtypeStruct((self.chips * rows, cols), pieces[0].dtype),
            cost_estimate=pl.CostEstimate(flops=0, bytes_accessed=4 * self.chips * rows * cols, transcendentals=0),
            name="lay_out",
        )(jnp.stack(places), *pieces)

    def scatter_sum(self, values):
        split = [value.reshape(self.chips, -1, value.shape[1]) for value in values]

        def join(offset, came=None):
            parts = [lax.dynamic_index_in_dim(value, self.chip_at(offset), 0, keepdims=False) for value in split]
            total = sum(part.astype(F32) for part in parts)
            return total if came is None else total + came.astype(F32)

        far = self.chips // 2
        up, down = join(far).astype(BF16), join(1 - far).astype(BF16)
        sent = []
        for step in range(far - 1, 0, -1):
            up, down = lax.ppermute(up, "chip", self.ahead), lax.ppermute(down, "chip", self.back)
            up, down = lax.optimization_barrier((up, down))
            up = join(step, up).astype(BF16)
            if step > 1:
                down = join(1 - step, down).astype(BF16)
            sent.append(up)
        last = lax.ppermute(up, "chip", self.ahead)
        return (lambda ready: join(0, after(down, ready)) + after(last, ready).astype(F32)), sent


def owner_rows(value):
    value = value.astype(F32)
    rows = value.shape[0] // 2
    mine, other = own_half((value[:rows], value[rows:]))
    return by_core(mine, swap(other, "core"))


def all_sum(value, axis, size):
    step = size // 2
    while step:
        came = lax.ppermute(value, axis, [(at, at ^ step) for at in range(size)])
        value = value + came
        step = step // 2
    return value


def local(chips, *args):
    return layer(chips, *args)


def layer(chips, tokens, norm_gain1, w_query, w_key, w_value, w_gate, w_decay, w_write, conv_query, conv_key,
          conv_value, a_log, dt_bias, out_gain, w_out, norm_gain2, w_ffgate, w_ffup, w_ffdown, cotangent):
    ring = Ring(chips)
    heads_n = a_log.shape[0] // 2
    ff = w_ffgate.shape[1] // 2
    tokens_o = swap(tokens, "tensor")
    cot_o = swap(cotangent, "tensor")

    pad = jnp.zeros((w_query.shape[0], 128 - 2 * heads_n), BF16)
    mix_parts = [
        jnp.concatenate(list(parts) + [pad], axis=1)
        for parts in zip(*map(halves, (w_out.T, w_query, w_key, w_value, w_gate, w_decay, w_write)))
    ]
    ffn_rows = chip_rows([
        jnp.concatenate(parts, axis=1)
        for parts in zip(*(wide_halves(value, FF_HALF) for value in (w_ffgate, w_ffup, w_ffdown.T)))
    ])
    w_mix = [ring.gather(chip_rows(mix_parts), ring.by_slices)]
    w_mix.append(swap(w_mix[0], "core"))
    w_ffn = [ring.gather(after(ffn_rows, w_mix[0]), ring.by_copies)]
    w_ffn.append(swap(w_ffn[0], "core"))
    val_w = heads_n * DV

    tokens32 = jnp.concatenate([tokens, tokens_o], axis=0).astype(F32)
    factor1 = row_factor(tokens32)
    unit1 = tokens32 * factor1
    normed1 = (unit1 * norm_gain1).astype(BF16)
    gain = out_gain.reshape(1, -1)
    params = []
    sides = [own_half(halves(value)) for value in (conv_query, conv_key, conv_value, a_log, dt_bias)]
    for cq, ck, cv, rate, bias in zip(*sides):
        heads_in = jnp.pad(jnp.stack([rate, bias]), ((0, 6), (0, 128 - heads_n)))
        params.append((cq, ck, cv, heads_in, gain))

    mixed = {}

    def mix(normed, seq, side):
        mixed[seq, side] = mix_forward(normed, w_mix[side], seq, params[side])

    def out_part(seq):
        return against_rows(mixed[seq, 0][0], w_mix[0][:, :val_w]) + against_rows(mixed[seq, 1][0], w_mix[1][:, :val_w])

    mix(normed1, 1, 0)
    mix(after(normed1, mixed[1, 0][0]), 1, 1)
    part_o = out_part(1).astype(BF16)
    came_s = swap(part_o, "tensor")
    mix(after(normed1, part_o), 0, 0)
    mix(after(normed1, mixed[0, 0][0]), 0, 1)
    resid1 = tokens32[:LEN] + out_part(0) + came_s.astype(F32)
    factor2 = row_factor(resid1)
    unit2 = resid1 * factor2
    normed2_s = (unit2 * norm_gain2).astype(BF16)
    normed2_o = swap(normed2_s, "tensor")

    *units, part_s, back_s = ffn_both(normed2_s, cotangent, w_ffn[0], w_ffn[1], 0, 2 * LEN, F32)
    *units, part_low, back_low = ffn_both(normed2_o, cot_o, w_ffn[0], w_ffn[1], 1, 2 * LEN, BF16, units)
    grad_rows2 = back_s + swap(back_low, "tensor").astype(F32)
    normed2, cot = (normed2_s, after(normed2_o, back_low)), (cotangent, cot_o)
    late_sent = late_grads(normed2, cot, units[3:])
    late_came = swap(late_sent, "core")
    late_own = late_grads((normed2_s, after(normed2_o, late_sent)), cot, units[:3])
    grad_resid = cotangent.astype(F32) + norm_backward(unit2, factor2, norm_gain2, grad_rows2)
    resid_s = after(grad_resid.astype(BF16), late_own)
    resid_o = swap(resid_s, "tensor")
    resid_rows = (resid_s, resid_o)
    result = resid1 + part_s + swap(after(part_low, resid_o), "tensor").astype(F32)
    late_last, _ = ring.scatter_sum([late_own, late_came])

    cols = w_mix[0].shape[1] - val_w
    grad_proj, small = [None, None], [None, None]
    ready = late_own
    for step, (seq, side) in enumerate(((0, 1), (0, 0), (1, 1), (1, 0))):
        grad_proj[side], sums = mix_backward(
            after(resid_rows[seq], ready), w_mix[side], seq, params[side], mixed[seq, side][1:], cols,
            grad_proj[side]
        )
        ready = grad_proj[side]
        small[side] = sums if seq == 0 else small[side] + sums
        if step == 2:
            ready = mix_grads(resid_rows, (mixed[0, 1][0], mixed[1, 1][0]), normed1, grad_proj[1])
            mix_came = swap(ready, "core")
    mix_own = mix_grads(resid_rows, (mixed[0, 0][0], mixed[1, 0][0]), normed1, grad_proj[0], mix_came)
    mix_last, mix_sent = ring.scatter_sum([mix_own])
    late_sum = owner_rows(late_last(mix_own))
    grad_proj[0] = after(grad_proj[0], mix_own)

    _, back_sent, gain_o = back_rows(grad_proj, w_mix, unit1, 1)
    mix_sum = owner_rows(mix_last(back_sent))
    back_s, _, gain_s = back_rows(grad_proj, w_mix, unit1, 0)
    grad_gain1 = gain_o[0] + gain_s[0]
    came_back = swap(back_sent, "tensor")
    last_parts = (came_back, back_s, unit1[:LEN], factor1[:LEN])
    came_back, back_s, unit_s, factor_s, *_ = lax.optimization_barrier((*last_parts, *mix_sent[-1:]))
    grad_rows1 = back_s + came_back.astype(F32)
    grad_tokens = grad_resid + norm_backward(unit_s, factor_s, norm_gain1, grad_rows1)

    grad_gain2 = jnp.sum(grad_rows2 * unit2, axis=0)
    head_rows = jnp.concatenate(by_core(small[0][0], small[1][0]), axis=0)
    out_gain_row = jnp.sum(head_rows[:, 8], axis=0, keepdims=True)
    wide = jnp.concatenate(
        [grad_gain1.reshape(-1, DV), grad_gain2.reshape(-1, DV), out_gain_row, head_rows.reshape(-1, DV)], axis=0
    )
    wide = all_sum(all_sum(wide, "chip", chips), "core", 2)
    count = grad_gain1.shape[0] // DV
    gains = all_sum(wide[: 2 * count + 1], "tensor", 2)
    head_rows = wide[2 * count + 1 :].reshape(2 * heads_n, 16, DV)

    def taps(rows):
        return jnp.transpose(rows, (1, 0, 2)).reshape(4, -1)

    def columns(parts, start, size):
        return jnp.concatenate([part[:, start : start + size] for part in parts], axis=1)

    key_w = heads_n * DK
    at = [0, val_w, val_w + key_w, val_w + 2 * key_w, 2 * val_w + 2 * key_w, 3 * val_w + 2 * key_w]
    return (
        result.astype(BF16),
        grad_tokens,
        gains[:count].reshape(-1),
        columns(mix_sum, at[1], key_w),
        columns(mix_sum, at[2], key_w),
        columns(mix_sum, at[3], val_w),
        columns(mix_sum, at[4], val_w),
        columns(mix_sum, at[5], heads_n),
        columns(mix_sum, at[5] + heads_n, heads_n),
        taps(head_rows[:, 4:8, :DK]),
        taps(head_rows[:, 4:8, DK:]),
        taps(head_rows[:, :4]),
        head_rows[:, 9, 0],
        head_rows[:, 9, 1],
        gains[2 * count],
        columns(mix_sum, at[0], val_w).T,
        gains[count : 2 * count].reshape(-1),
        columns(late_sum, 0, ff),
        columns(late_sum, FF_HALF, ff),
        columns(late_sum, 2 * FF_HALF, ff).T,
    )


def solution(mesh):
    chips = mesh.shape["dp"] // 2
    inner = jax.sharding.Mesh(mesh.devices.reshape(chips, 2, -1), ("chip", "core", "tensor"))
    dp, rows, every = ("chip", "core"), P(("chip", "core", "tensor"), None), P()
    down, across, taps, head = P(dp, "tensor"), P("tensor", dp), P(None, "tensor"), P("tensor")
    return jax.shard_map(
        functools.partial(local, chips),
        mesh=inner,
        in_specs=(rows, every, down, down, down, down, down, down, taps, taps, taps, head, head, every, across, every,
                  down, down, across, rows),
        out_specs=(rows, rows, every, down, down, down, down, down, down, taps, taps, taps, head, head, every, across,
                   every, down, down, across),
        check_vma=False,
    )
```

```python
import functools
import math

import jax
import jax.numpy as jnp
from jax import lax
from jax.experimental import pallas as pl
from jax.experimental.pallas import tpu as pltpu
from jax.sharding import PartitionSpec as P


F32 = jnp.float32
BF16 = jnp.bfloat16
LEN = 512
DK = 128
DV = 256
CHUNK = 128
FF_HALF = 768
PARTS = LEN // CHUNK


def dot_nn(a, b):
    return lax.dot_general(a, b, (((1,), (0,)), ((), ())), preferred_element_type=F32)


def dot_nt(a, b):
    return lax.dot_general(a, b, (((1,), (1,)), ((), ())), preferred_element_type=F32)


def dot_tn(a, b):
    return lax.dot_general(a, b, (((0,), (0,)), ((), ())), preferred_element_type=F32)


def sigmoid(x):
    return 1.0 / (1.0 + jnp.exp(-x))


def softplus(x):
    return jnp.maximum(x, 0.0) + jnp.log1p(jnp.exp(-jnp.abs(x)))


def exact_rows(rows, ones):
    first = rows.astype(BF16)
    rest = rows - first.astype(F32)
    second = rest.astype(BF16)
    third = (rest - second.astype(F32)).astype(BF16)
    return dot_nn(first, ones) + dot_nn(second, ones) + dot_nn(third, ones)


def iota2(rows, cols, axis):
    return lax.broadcasted_iota(jnp.int32, (rows, cols), axis)


def same_group(size):
    shift = size.bit_length() - 1
    return (iota2(CHUNK, CHUNK, 0) >> shift) == (iota2(CHUNK, CHUNK, 1) >> shift)


def tri(upper):
    row, col = iota2(CHUNK, CHUNK, 0), iota2(CHUNK, CHUNK, 1)
    keep = row <= col if upper else row >= col
    return keep.astype(F32).astype(BF16)


def spread(row):
    return jnp.broadcast_to(row, (CHUNK, CHUNK)).T


def twice(x):
    return jnp.concatenate([x, x], axis=1)


def odd_blocks(x, size):
    return jnp.concatenate([x[at : at + size] for at in range(size, CHUNK, 2 * size)], axis=0)


def weave(even, odd, size):
    parts = []
    for at in range(0, CHUNK // 2, size):
        parts += [even[at : at + size], odd[at : at + size]]
    return jnp.concatenate(parts, axis=0)


def invert_all(lowers):
    in8 = same_group(8)
    lane = iota2(8, CHUNK, 1) & 7
    place = iota2(8, CHUNK, 0)
    small = [jnp.sum(jnp.where(in8, lower, 0.0).reshape(CHUNK // 8, 8, CHUNK), axis=0) for lower in lowers]
    masked = [jnp.where(lane == at, member, 0.0) for member in small for at in range(7)]
    columns = dot_nn(jnp.concatenate(masked, axis=0).astype(BF16), in8.astype(F32).astype(BF16))
    inverse = []
    for which in range(len(lowers)):
        solved = jnp.where(lane == place, 1.0, 0.0)
        for at in range(7):
            start = (which * 7 + at) * 8
            solved = solved - columns[start : start + 8] * jnp.broadcast_to(solved[at : at + 1], (8, CHUNK))
        inverse.append(jnp.where(in8, jnp.concatenate([solved] * (CHUNK // 8), axis=0), 0.0))
    size = 8
    while size < CHUNK:
        ring = jnp.logical_and(same_group(2 * size), jnp.logical_not(same_group(size)))
        between = [odd_blocks(jnp.where(ring, lower, 0.0), size).astype(BF16) for lower in lowers]
        low = [member.astype(BF16) for member in inverse]
        inner = [dot_nn(a, b) for a, b in zip(between, low)]
        padded = [weave(jnp.zeros_like(member), member, size).astype(BF16) for member in inner]
        odd = [odd_blocks(member, size) for member in inverse]
        new_odd = [a - dot_nn(a.astype(BF16), b) for a, b in zip(odd, padded)]
        even = [
            jnp.concatenate([member[at : at + size] for at in range(0, CHUNK, 2 * size)], axis=0) for member in inverse
        ]
        inverse = [weave(a, b, size) for a, b in zip(even, new_odd)]
        size *= 2
    return [member.astype(BF16) for member in inverse]


def head_value(heads_ref, row, head):
    values = heads_ref[row : row + 1, :]
    lane = lax.broadcasted_iota(jnp.int32, values.shape, 1)
    return jnp.sum(jnp.where(lane == head, values, 0.0), axis=1, keepdims=True)


def head_rates(ab_ref, heads_ref, head, heads_n):
    decay_in = ab_ref[pl.ds(head, 1), :] + head_value(heads_ref, 1, head)
    write = sigmoid(ab_ref[pl.ds(heads_n + head, 1), :])
    rate = -jnp.exp(head_value(heads_ref, 0, head))
    soft = softplus(decay_in)
    decay = rate * soft
    rows = [decay[:, at * CHUNK : (at + 1) * CHUNK] for at in range(PARTS)]
    stacked = jnp.concatenate(rows + [jnp.zeros((8 - PARTS, CHUNK), F32)], axis=0)
    return write, decay_in, rate, soft, exact_rows(stacked, tri(True))


def convolve(ref, part, taps):
    body = ref[pl.ds(part * CHUNK, CHUNK), :]
    if part == 0:
        head = jnp.zeros((8, body.shape[1]), F32)
    else:
        head = ref[pl.ds(part * CHUNK - 8, 8), :]
    rows = jnp.concatenate([head, body], axis=0)
    total = body * taps[3:4, :]
    for tap in range(3):
        total = total + rows[5 + tap : 5 + tap + CHUNK, :] * taps[tap : tap + 1, :]
    return total


def chunk_core(xq, xk, xv, write_row, total_row):
    row, col = iota2(CHUNK, CHUNK, 0), iota2(CHUNK, CHUNK, 1)
    gq, gk, gv = sigmoid(xq), sigmoid(xk), sigmoid(xv)
    sq, sk, values = xq * gq, xk * gk, xv * gv
    rq = lax.rsqrt(jnp.sum(sq * sq, axis=1, keepdims=True) + 1e-06)
    rk = lax.rsqrt(jnp.sum(sk * sk, axis=1, keepdims=True) + 1e-06)
    queries = sq * (rq * (1.0 / math.sqrt(DK)))
    keys = sk * rk
    q_low, k_low = queries.astype(BF16), keys.astype(BF16)
    write, total = spread(write_row), spread(total_row)
    fade = jnp.where(row >= col, jnp.exp(jnp.minimum(total - total_row, 0.0)), 0.0)
    fade_strict = jnp.where(row > col, fade, 0.0)
    key_inner = dot_nt(k_low, k_low)
    last_row = total_row[:, CHUNK - 1 : CHUNK]
    from_start = jnp.exp(total)
    to_end = jnp.exp(last_row - total)
    return dict(
        gq=gq, gk=gk, gv=gv, rq=rq, rk=rk, queries=queries, keys=keys, values=values, q_low=q_low, k_low=k_low,
        write=write, fade=fade, fade_strict=fade_strict, key_inner=key_inner, scores=dot_nt(q_low, k_low) * fade,
        lower=write * key_inner * fade_strict, from_start=from_start, to_end=to_end, last=jnp.exp(last_row),
        key_start=(write * from_start) * keys, q_start=queries * from_start, key_end=keys * to_end,
    )


def forward_kernel(heads_n, x_ref, wq_ref, wk_ref, wv_ref, wg_ref, wab_ref, cq_ref, ck_ref, cv_ref, heads_ref,
                   gain_ref, gated_ref, mixed_ref, delta_ref, solve_ref, state_ref, pq_ref, pk_ref, pv_ref, pg_ref,
                   xq_ref, xk_ref, xv_ref, ab_ref, turned):
    head = pl.program_id(0)

    @pl.when(head == 0)
    def _():
        turned[...] = dot_nn(x_ref[...], wab_ref[...]).T
        ab_ref[...] = turned[0:8, :]

    pq_ref[...] = dot_nn(x_ref[...], wq_ref[...])
    pk_ref[...] = dot_nn(x_ref[...], wk_ref[...])
    pv_ref[...] = dot_nn(x_ref[...], wv_ref[...])
    pg_ref[...] = dot_nn(x_ref[...], wg_ref[...])
    gain = gain_ref[0:1, :]
    write, _, _, _, totals = head_rates(turned, heads_ref, head, heads_n)
    cores = []
    for part in range(PARTS):
        span = pl.ds(part * CHUNK, CHUNK)
        xs = [convolve(ref, part, taps[...]) for ref, taps in ((pq_ref, cq_ref), (pk_ref, ck_ref), (pv_ref, cv_ref))]
        for ref, value in zip((xq_ref, xk_ref, xv_ref), xs):
            ref[span, :] = value
        cores.append(chunk_core(*xs, write[:, part * CHUNK : (part + 1) * CHUNK], totals[part : part + 1, :]))
    solves = invert_all([core["lower"] for core in cores])
    for part in range(PARTS):
        solve_ref[0, 0, part] = solves[part]
    value_parts = [dot_nn(t, (twice(c["write"]) * c["values"]).astype(BF16)) for t, c in zip(solves, cores)]
    key_parts = [dot_nn(t, c["key_start"].astype(BF16)).astype(BF16) for t, c in zip(solves, cores)]
    state = jnp.zeros((DK, DV), F32)
    for part in range(PARTS):
        core = cores[part]
        state_low = state.astype(BF16)
        state_ref[0, 0, part] = state_low
        update = value_parts[part] - dot_nn(key_parts[part], state_low)
        update_low = update.astype(BF16)
        mixed = dot_nn(core["q_start"].astype(BF16), state_low) + dot_nn(core["scores"].astype(BF16), update_low)
        if part < PARTS - 1:
            state = core["last"] * state + dot_tn(core["key_end"].astype(BF16), update_low)
        span = pl.ds(part * CHUNK, CHUNK)
        delta_ref[span, :] = update_low
        mixed_ref[span, :] = mixed.astype(BF16)
        factor = lax.rsqrt(jnp.mean(mixed * mixed, axis=1, keepdims=True) + 1e-05)
        gate_in = pg_ref[span, :]
        gated_ref[span, :] = (mixed * factor * gain * (gate_in * sigmoid(gate_in))).astype(BF16)


def backward_kernel(heads_n, resid_ref, wo_ref, cq_ref, ck_ref, cv_ref, heads_ref, gain_ref, mixed_ref, delta_ref,
                    solve_ref, state_ref, pq_ref, pk_ref, pv_ref, pg_ref, xq_ref, xk_ref, xv_ref, ab_ref, *refs):
    dp_ref, small_ref, grad_ref, turned = refs[-4:]
    head = pl.program_id(0)
    row, col = iota2(CHUNK, CHUNK, 0), iota2(CHUNK, CHUNK, 1)
    gain = gain_ref[0:1, :]
    width_k, width_v = heads_n * DK, heads_n * DV
    scale = 1.0 / math.sqrt(DK)

    def fold(x):
        return jnp.sum(x.reshape(CHUNK // 8, 8, x.shape[1]), axis=0)

    def down(x):
        return jnp.sum(x, axis=0, keepdims=True)

    @pl.when(head == 0)
    def _():
        turned[...] = jnp.zeros_like(turned)

    grad_ref[...] = dot_nn(resid_ref[...], wo_ref[...])
    write_row, decay_in, rate, soft, totals = head_rates(ab_ref, heads_ref, head, heads_n)
    state_grad = jnp.zeros((DK, DV), F32)
    gain_sum = jnp.zeros((8, DV), F32)
    taps_sum = {name: [jnp.zeros((8, size), F32) for _ in range(4)] for name, size in (("q", DK), ("k", DK), ("v", DV))}
    following = {"q": jnp.zeros((8, DK), F32), "k": jnp.zeros((8, DK), F32), "v": jnp.zeros((8, DV), F32)}
    rate_sum = jnp.zeros((1, CHUNK), F32)
    bias_sum = jnp.zeros((1, CHUNK), F32)
    suffix, which = tri(False), iota2(8, CHUNK, 0)
    for part in reversed(range(PARTS)):
        span = pl.ds(part * CHUNK, CHUNK)
        piece = slice(part * CHUNK, (part + 1) * CHUNK)
        xq, xk, xv = xq_ref[span, :], xk_ref[span, :], xv_ref[span, :]
        core = chunk_core(xq, xk, xv, write_row[:, piece], totals[part : part + 1, :])
        write, keys, queries, values = core["write"], core["keys"], core["queries"], core["values"]
        k_low, q_low, fade = core["k_low"], core["q_low"], core["fade"]
        solve, state_low, delta = solve_ref[0, 0, part], state_ref[0, 0, part], delta_ref[span, :]
        mixed = mixed_ref[span, :].astype(F32)
        factor = lax.rsqrt(jnp.mean(mixed * mixed, axis=1, keepdims=True) + 1e-05)
        normed = mixed * factor
        gate_in = pg_ref[span, :]
        gate_sig = sigmoid(gate_in)
        gate = gate_in * gate_sig
        grad = grad_ref[span, :]
        plain = grad * normed
        gain_sum = gain_sum + fold(plain * gate)
        dp_ref[span, pl.ds(pl.multiple_of(2 * width_k + width_v + head * DV, DV), DV)] = (
            plain * gain * (gate_sig + gate * (1.0 - gate_sig))
        ).astype(BF16)
        normed_grad = grad * gate * gain
        mixed_grad = factor * (normed_grad - normed * jnp.mean(normed_grad * normed, axis=1, keepdims=True))
        mixed_low = mixed_grad.astype(BF16)
        key_part = dot_nn(solve, core["key_start"].astype(BF16)).astype(BF16)
        grad_low = state_grad.astype(BF16)
        update_grad = dot_tn(core["scores"].astype(BF16), mixed_low) + dot_nn(core["key_end"].astype(BF16), grad_low)
        update_low = update_grad.astype(BF16)
        key_end_grad = dot_nt(delta, grad_low)
        last_grad = jnp.sum(state_low.astype(F32) * state_grad)
        if part > 0:
            state_grad = (
                core["last"] * state_grad
                + dot_tn(core["q_start"].astype(BF16), mixed_low)
                - dot_tn(key_part, update_low)
            )
        q_start_grad = dot_nt(mixed_low, state_low)
        scores_grad = dot_nt(mixed_low, delta)
        right_grad = dot_tn(solve, update_low)
        right_low = right_grad.astype(BF16)
        lower_grad = jnp.where(row > col, -dot_nt(right_low, delta), 0.0)
        key_start_grad = -dot_nt(right_low, state_low)
        inner_low = (scores_grad * fade).astype(BF16)
        queries_grad = q_start_grad * core["from_start"] + dot_nn(inner_low, k_low)
        faded_lower = lower_grad * core["fade_strict"]
        key_inner_grad = write * faded_lower
        both = (key_inner_grad + key_inner_grad.T).astype(BF16)
        keys_grad = (
            key_end_grad * core["to_end"]
            + key_start_grad * (write * core["from_start"])
            + dot_tn(inner_low, q_low)
            + dot_nn(both, k_low)
        )
        values_grad = twice(write) * right_grad
        start_keys = key_start_grad * core["from_start"] * keys
        value_terms = right_grad * values
        write_grad = down(
            (start_keys + faded_lower * core["key_inner"] + value_terms[:, :CHUNK] + value_terms[:, CHUNK:]).T
        )
        ends = key_end_grad * core["key_end"]
        gaps_grad = scores_grad * core["scores"] + lower_grad * core["lower"]
        total_grad = down((q_start_grad * core["q_start"] + write * start_keys - ends + gaps_grad).T) - down(gaps_grad)
        at_end = jnp.sum(ends) + last_grad * core["last"]
        decay_grad = exact_rows(jnp.broadcast_to(total_grad, (8, CHUNK)), suffix)[0:1, :] + at_end
        rate_sum = rate_sum + decay_grad * (rate * soft[:, piece])
        decay_in_grad = decay_grad * (rate * sigmoid(decay_in[:, piece]))
        bias_sum = bias_sum + decay_in_grad
        write_in_grad = write_grad * (write_row[:, piece] * (1.0 - write_row[:, piece]))
        held = jnp.where(which == head, decay_in_grad, turned[0:8, span])
        turned[0:8, span] = jnp.where(which == heads_n + head, write_in_grad, held)
        unit = queries * (1.0 / scale)
        sq_grad = (core["rq"] * scale) * (
            queries_grad - unit * jnp.sum(queries_grad * unit, axis=1, keepdims=True)
        )
        sk_grad = core["rk"] * (keys_grad - keys * jnp.sum(keys_grad * keys, axis=1, keepdims=True))
        for name, grad_in, x, sig, p_ref, taps_ref, start, size in (
            ("q", sq_grad, xq, core["gq"], pq_ref, cq_ref, 0, DK),
            ("k", sk_grad, xk, core["gk"], pk_ref, ck_ref, width_k, DK),
            ("v", values_grad, xv, core["gv"], pv_ref, cv_ref, 2 * width_k, DV),
        ):
            taps, rows = taps_ref[...], p_ref[span, :]
            x_grad = grad_in * (sig + x * sig * (1.0 - sig))
            longer = jnp.concatenate([x_grad, following[name]], axis=0)
            following[name] = x_grad[0:8, :]
            taps_sum[name][3] = taps_sum[name][3] + fold(rows * x_grad)
            proj = x_grad * taps[3:4, :]
            for tap in range(3):
                moved = longer[3 - tap : 3 - tap + CHUNK, :]
                taps_sum[name][tap] = taps_sum[name][tap] + fold(rows * moved)
                proj = proj + moved * taps[tap : tap + 1, :]
            dp_ref[span, pl.ds(pl.multiple_of(start + head * size, size), size)] = proj.astype(BF16)

    @pl.when(head == heads_n - 1)
    def _():
        dp_ref[:, pl.ds(2 * width_k + 2 * width_v, 128)] = turned[...].T.astype(BF16)

    lane = iota2(1, DV, 1)
    rates, biases = jnp.sum(rate_sum, axis=1, keepdims=True), jnp.sum(bias_sum, axis=1, keepdims=True)
    small = [down(taps_sum["v"][tap]) for tap in range(4)]
    small += [jnp.concatenate([down(taps_sum["q"][tap]), down(taps_sum["k"][tap])], axis=1) for tap in range(4)]
    small += [down(gain_sum), jnp.where(lane == 0, rates, 0.0) + jnp.where(lane == 1, biases, 0.0)]
    small += [jnp.zeros((6, DV), F32)]
    small_ref[0, 0] = jnp.concatenate(small, axis=0)


def param_specs():
    return [
        pl.BlockSpec((4, DK), lambda h: (0, h)),
        pl.BlockSpec((4, DK), lambda h: (0, h)),
        pl.BlockSpec((4, DV), lambda h: (0, h)),
        pl.BlockSpec((8, 128), lambda h: (0, 0)),
        pl.BlockSpec((1, DV), lambda h: (0, 0)),
    ]


def saved_specs():
    narrow, wide = pl.BlockSpec((LEN, DK), lambda h: (0, h)), pl.BlockSpec((LEN, DV), lambda h: (0, h))
    return [
        wide, wide,
        pl.BlockSpec((1, 1, PARTS, CHUNK, CHUNK), lambda h: (0, h, 0, 0, 0)),
        pl.BlockSpec((1, 1, PARTS, DK, DV), lambda h: (0, h, 0, 0, 0)),
        narrow, narrow, wide, wide, narrow, narrow, wide,
        pl.BlockSpec((8, LEN), lambda h: (0, 0)),
    ]


def mix_forward(normed, weights, seq, params):
    width, heads_n = normed.shape[1], params[0].shape[1] // DK
    col_q, col_v = heads_n * DV // DK, heads_n + 2 * heads_n * DK // DV

    def shape(*dims, kind=F32):
        return jax.ShapeDtypeStruct(dims, kind)

    low = shape(LEN, heads_n * DV, kind=BF16)
    narrow, wide = shape(LEN, heads_n * DK), shape(LEN, heads_n * DV)
    return pl.pallas_call(
        functools.partial(forward_kernel, heads_n),
        grid=(heads_n,),
        in_specs=[
            pl.BlockSpec((LEN, width), lambda h: (seq, 0)),
            pl.BlockSpec((width, DK), lambda h: (0, col_q + h)),
            pl.BlockSpec((width, DK), lambda h: (0, col_q + heads_n + h)),
            pl.BlockSpec((width, DV), lambda h: (0, col_v + h)),
            pl.BlockSpec((width, DV), lambda h: (0, col_v + heads_n + h)),
            pl.BlockSpec((width, 128), lambda h: (0, col_q + 6 * heads_n)),
        ] + param_specs(),
        out_specs=[pl.BlockSpec((LEN, DV), lambda h: (0, h))] + saved_specs(),
        out_shape=[
            low, low, low,
            shape(1, heads_n, PARTS, CHUNK, CHUNK, kind=BF16),
            shape(1, heads_n, PARTS, DK, DV, kind=BF16),
            narrow, narrow, wide, wide, narrow, narrow, wide,
            shape(8, LEN),
        ],
        scratch_shapes=[pltpu.VMEM((128, LEN), F32)],
        cost_estimate=pl.CostEstimate(flops=3 * 10**9 * heads_n, bytes_accessed=5 * 10**6 * heads_n, transcendentals=10**6),
        name="mix_forward",
    )(normed, *[weights] * 5, *params)


def mix_backward(resid, w_out, seq, params, saved, cols, earlier=None):
    heads_n, width = params[0].shape[1] // DK, resid.shape[1]
    held = [earlier] if earlier is not None else []
    return pl.pallas_call(
        functools.partial(backward_kernel, heads_n),
        grid=(heads_n,),
        in_specs=[pl.BlockSpec((LEN, width), lambda h: (0, 0)), pl.BlockSpec((width, DV), lambda h: (0, h))]
        + param_specs() + saved_specs() + [pl.BlockSpec(memory_space=pl.ANY)] * len(held),
        out_specs=[
            pl.BlockSpec((LEN, cols), lambda h: (seq, 0)),
            pl.BlockSpec((1, 1, 16, DV), lambda h: (0, h, 0, 0)),
        ],
        out_shape=[
            jax.ShapeDtypeStruct((2 * LEN, cols), BF16),
            jax.ShapeDtypeStruct((1, heads_n, 16, DV), F32),
        ],
        scratch_shapes=[pltpu.VMEM((LEN, DV), F32), pltpu.VMEM((128, LEN), F32)],
        input_output_aliases={19: 0} if held else {},
        cost_estimate=pl.CostEstimate(flops=5 * 10**9 * heads_n, bytes_accessed=6 * 10**6 * heads_n, transcendentals=10**6),
        name="mix_backward",
    )(resid, w_out, *params, *saved, *held)


def ffn_kernel(held, x_ref, cot_ref, mine_ref, other_ref, *refs):
    outs, (w_ref, part_sum, back_sum, sems) = refs[held : held + 8], refs[held + 8 :]
    part_ref, back_ref = outs[6], outs[7]
    units = w_ref.shape[2]
    copies = []
    for half, source in enumerate((mine_ref, other_ref)):
        for at in range(3):
            slot = 3 * half + at
            copies.append(
                pltpu.make_async_copy(source.at[:, pl.ds(at * units, units)], w_ref.at[slot], sems.at[slot])
            )
    for copy in copies:
        copy.start()
    for half in range(2):
        at = 3 * half
        copies[at].wait()
        gate = dot_nn(x_ref[...], w_ref[at])
        copies[at + 1].wait()
        up = dot_nn(x_ref[...], w_ref[at + 1])
        copies[at + 2].wait()
        grad = dot_nn(cot_ref[...], w_ref[at + 2])
        sig = sigmoid(gate)
        act = gate * sig
        outs[at][...] = (act * up).astype(BF16)
        outs[at + 1][...] = (grad * up * (sig + act * (1.0 - sig))).astype(BF16)
        outs[at + 2][...] = (grad * act).astype(BF16)
        part = dot_nt(outs[at][...], w_ref[at + 2])
        back = dot_nt(outs[at + 1][...], w_ref[at]) + dot_nt(outs[at + 2][...], w_ref[at + 1])
        if half == 0:
            part_sum[...] = part
            back_sum[...] = back
        else:
            part_ref[...] = (part_sum[...] + part).astype(part_ref.dtype)
            back_ref[...] = (back_sum[...] + back).astype(back_ref.dtype)


def ffn_both(x, cot, mine, other, seq, total, kind, earlier=None):
    rows, width = x.shape
    units = FF_HALF
    whole = pl.BlockSpec((rows, width), lambda i: (0, 0))
    anywhere = pl.BlockSpec(memory_space=pl.ANY)
    tiles = pl.BlockSpec((rows, units), lambda i: (seq, 0))
    held = list(earlier) if earlier else []
    return pl.pallas_call(
        functools.partial(ffn_kernel, len(held)),
        grid=(1,),
        in_specs=[whole, whole, anywhere, anywhere] + [anywhere] * len(held),
        out_specs=[tiles] * 6 + [whole, whole],
        out_shape=[jax.ShapeDtypeStruct((total, units), BF16)] * 6 + [jax.ShapeDtypeStruct((rows, width), kind)] * 2,
        input_output_aliases={4 + at: at for at in range(len(held))},
        scratch_shapes=[pltpu.VMEM((6, width, units), BF16)] + [pltpu.VMEM((rows, width), F32)] * 2
        + [pltpu.SemaphoreType.DMA((6,))],
        cost_estimate=pl.CostEstimate(flops=24 * rows * width * units, bytes_accessed=25 * 10**6, transcendentals=rows * units * 2),
        name="ffn_both",
    )(x, cot, mine, other, *held)


def late_kernel(normed_s, normed_o, cot_s, cot_o, gate_ref, up_ref, hidden_ref, out_ref):
    size = hidden_ref.shape[1]
    normed = jnp.concatenate([normed_s[...].T, normed_o[...].T], axis=1)
    cot = jnp.concatenate([cot_s[...].T, cot_o[...].T], axis=1)
    for at, (left, right) in enumerate(((normed, gate_ref), (normed, up_ref), (cot, hidden_ref))):
        out_ref[:, at * size : (at + 1) * size] = dot_nn(left, right[...]).astype(BF16)


def late_grads(normed, cot, units):
    hidden, grad_gate, grad_up = units
    (rows, size), width, tile = hidden.shape, cot[0].shape[1], 256
    return pl.pallas_call(
        late_kernel,
        grid=(width // tile,),
        in_specs=[pl.BlockSpec((LEN, tile), lambda i: (0, i))] * 4 + [pl.BlockSpec((rows, size), lambda i: (0, 0))] * 3,
        out_specs=pl.BlockSpec((tile, 3 * size), lambda i: (i, 0)),
        out_shape=jax.ShapeDtypeStruct((width, 3 * size), BF16),
        cost_estimate=pl.CostEstimate(flops=6 * rows * width * size, bytes_accessed=16 * 10**6, transcendentals=0),
        name="late_grads",
    )(*normed, *cot, grad_gate, grad_up, hidden)


def out_kernel(gated0_ref, gated1_ref, w0_ref, w1_ref, out_ref):
    out_ref[...] = (dot_nt(gated0_ref[...], w0_ref[...]) + dot_nt(gated1_ref[...], w1_ref[...])).astype(BF16)


def out_rows(gated, weights, width):
    (rows, size), tile = gated[0].shape, 256
    return pl.pallas_call(
        out_kernel,
        grid=(rows // tile,),
        in_specs=[pl.BlockSpec((tile, size), lambda i: (i, 0))] * 2 + [pl.BlockSpec((width, size), lambda i: (0, 0))] * 2,
        out_specs=pl.BlockSpec((tile, width), lambda i: (i, 0)),
        out_shape=jax.ShapeDtypeStruct((rows, width), BF16),
        cost_estimate=pl.CostEstimate(flops=4 * rows * width * size, bytes_accessed=4 * 10**6, transcendentals=0),
        name="out_rows",
    )(*gated, *weights)


def resid_kernel(gated0_ref, gated1_ref, w0_ref, w1_ref, tokens_ref, came_ref, gain_ref, resid_ref, normed_ref):
    resid = dot_nt(gated0_ref[...], w0_ref[...]) + dot_nt(gated1_ref[...], w1_ref[...])
    resid = tokens_ref[...].astype(F32) + (resid + came_ref[...].astype(F32))
    factor = lax.rsqrt(jnp.mean(resid * resid, axis=1, keepdims=True) + 1e-05)
    resid_ref[...] = resid
    normed_ref[...] = (resid * factor * gain_ref[...]).astype(BF16)


def resid_rows_of(gated, weights, tokens, came, gain):
    (rows, width), (_, size), tile = tokens.shape, gated[0].shape, 256
    wide = pl.BlockSpec((tile, width), lambda i: (i, 0))
    return pl.pallas_call(
        resid_kernel,
        grid=(rows // tile,),
        in_specs=[pl.BlockSpec((tile, size), lambda i: (i, 0))] * 2 + [pl.BlockSpec((width, size), lambda i: (0, 0))] * 2
        + [wide, wide, pl.BlockSpec((1, width), lambda i: (0, 0))],
        out_specs=[wide, wide],
        out_shape=[jax.ShapeDtypeStruct((rows, width), F32), jax.ShapeDtypeStruct((rows, width), BF16)],
        cost_estimate=pl.CostEstimate(flops=4 * rows * width * size, bytes_accessed=8 * 10**6, transcendentals=rows),
        name="resid_rows",
    )(*gated, *weights, tokens, came, gain)


def resid_back_kernel(resid_ref, back_ref, came_ref, cot_ref, gain_ref, grad_ref, low_ref, sum_ref):
    resid = resid_ref[...]
    factor = lax.rsqrt(jnp.mean(resid * resid, axis=1, keepdims=True) + 1e-05)
    unit = resid * factor
    rows = back_ref[...] + came_ref[...].astype(F32)
    inner = rows * gain_ref[...]
    grad = cot_ref[...].astype(F32) + factor * (inner - unit * jnp.mean(inner * unit, axis=1, keepdims=True))
    grad_ref[...] = grad
    low_ref[...] = grad.astype(BF16)
    part = jnp.sum(rows * unit, axis=0, keepdims=True)

    @pl.when(pl.program_id(0) == 0)
    def _():
        sum_ref[...] = part

    @pl.when(pl.program_id(0) > 0)
    def _():
        sum_ref[...] = sum_ref[...] + part


def resid_back(resid, back, came, cot, gain):
    (rows, width), tile = resid.shape, 128
    wide, flat = pl.BlockSpec((tile, width), lambda i: (i, 0)), pl.BlockSpec((1, width), lambda i: (0, 0))
    return pl.pallas_call(
        resid_back_kernel,
        grid=(rows // tile,),
        in_specs=[wide] * 4 + [flat],
        out_specs=[wide, wide, flat],
        out_shape=[jax.ShapeDtypeStruct((rows, width), F32), jax.ShapeDtypeStruct((rows, width), BF16),
                   jax.ShapeDtypeStruct((1, width), F32)],
        cost_estimate=pl.CostEstimate(flops=20 * rows * width, bytes_accessed=9 * 10**6, transcendentals=rows),
        name="resid_back",
    )(resid, back, came, cot, gain)


def mix_kernel(held, resid_s, resid_o, normed_ref, gated_s, gated_o, grad_ref, *refs):
    out_ref, split = refs[-1], gated_s.shape[1]
    first = dot_nn(resid_s[...].T, gated_s[...]) + dot_nn(resid_o[...].T, gated_o[...])
    second = dot_nn(normed_ref[...].T, grad_ref[...])
    if held:
        first = first + refs[0][:, :split].astype(F32)
        second = second + refs[0][:, split:].astype(F32)
    out_ref[:, :split] = first.astype(BF16)
    out_ref[:, split:] = second.astype(BF16)


def mix_grads(resid, gated, normed, grads, came=None):
    (rows, width), tile = normed.shape, 256
    cols = gated[0].shape[1] + grads.shape[1]
    down = pl.BlockSpec((tile, cols), lambda i: (i, 0))
    held = [came] if came is not None else []
    whole = [pl.BlockSpec(value.shape, lambda i: (0, 0)) for value in (*gated, grads)]
    return pl.pallas_call(
        functools.partial(mix_kernel, len(held)),
        grid=(width // tile,),
        in_specs=[pl.BlockSpec((LEN, tile), lambda i: (0, i))] * 2 + [pl.BlockSpec((rows, tile), lambda i: (0, i))]
        + whole + [down] * len(held),
        out_specs=down,
        out_shape=jax.ShapeDtypeStruct((width, cols), BF16),
        cost_estimate=pl.CostEstimate(flops=2 * rows * width * cols, bytes_accessed=14 * 10**6, transcendentals=0),
        name="mix_grads",
    )(*resid, normed, *gated, grads, *held)


def back_kernel(skip, mine_ref, other_ref, w0_ref, w1_ref, unit_ref, out_ref, low_ref, gain_ref):
    total = dot_nt(mine_ref[...], w0_ref[:, skip:]) + dot_nt(other_ref[...], w1_ref[:, skip:])
    out_ref[...] = total
    low_ref[...] = total.astype(BF16)
    gain_ref[...] = jnp.sum(total * unit_ref[...], axis=0, keepdims=True)


def back_rows(grads, weights, unit, seq):
    (width, all_cols), cols, tile = weights[0].shape, grads[0].shape[1], 256
    rows = pl.BlockSpec((LEN, cols), lambda i: (seq, 0))
    rights = pl.BlockSpec((tile, all_cols), lambda i: (i, 0))
    outs = pl.BlockSpec((LEN, tile), lambda i: (0, i))
    return pl.pallas_call(
        functools.partial(back_kernel, all_cols - cols),
        grid=(width // tile,),
        in_specs=[rows, rows, rights, rights, pl.BlockSpec((LEN, tile), lambda i: (seq, i))],
        out_specs=[outs, outs, pl.BlockSpec((1, tile), lambda i: (0, i))],
        out_shape=[
            jax.ShapeDtypeStruct((LEN, width), F32),
            jax.ShapeDtypeStruct((LEN, width), BF16),
            jax.ShapeDtypeStruct((1, width), F32),
        ],
        cost_estimate=pl.CostEstimate(flops=4 * LEN * width * cols, bytes_accessed=17 * 10**6, transcendentals=0),
        name="back_rows",
    )(*grads, *weights, unit)


def pack_kernel(cuts, core_ref, *refs):
    sources, outs = refs[: len(cuts)], refs[len(cuts) :]
    for out_ref, side in zip(outs, (core_ref[0], 1 - core_ref[0])):
        for source, (start, size) in zip(sources, cuts):
            out_ref[:, start : start + size] = source[:, pl.ds(pl.multiple_of(side * size, 128), size)]


def pack(core, values):
    cuts, at = [], 0
    for value in values:
        cuts.append((at, value.shape[1] // 2))
        at += value.shape[1] // 2
    rows = values[0].shape[0]
    return pl.pallas_call(
        functools.partial(pack_kernel, cuts),
        grid_spec=pltpu.PrefetchScalarGridSpec(
            num_scalar_prefetch=1,
            grid=(1,),
            in_specs=[pl.BlockSpec(value.shape, lambda i, core_ref: (0, 0)) for value in values],
            out_specs=[pl.BlockSpec((rows, at), lambda i, core_ref: (0, 0))] * 2,
        ),
        out_shape=[jax.ShapeDtypeStruct((rows, at), values[0].dtype)] * 2,
        cost_estimate=pl.CostEstimate(flops=0, bytes_accessed=8 * rows * at, transcendentals=0),
        name="pack",
    )(core, *values)


def unpack_kernel(cuts, core_ref, mine_ref, came_ref, *outs):
    for ref, side in ((mine_ref, core_ref[0]), (came_ref, 1 - core_ref[0])):
        for out_ref, (start, size) in zip(outs, cuts):
            out_ref[:, pl.ds(pl.multiple_of(side * size, 128), size)] = ref[:, start : start + size]


def unpack(core, mine, came, sizes):
    rows, cols = mine.shape
    cuts = [(sum(sizes[:at]), size) for at, size in enumerate(sizes)]
    return pl.pallas_call(
        functools.partial(unpack_kernel, cuts),
        grid_spec=pltpu.PrefetchScalarGridSpec(
            num_scalar_prefetch=1,
            grid=(1,),
            in_specs=[pl.BlockSpec((rows, cols), lambda i, core_ref: (0, 0))] * 2,
            out_specs=[pl.BlockSpec((rows, 2 * size), lambda i, core_ref: (0, 0)) for size in sizes],
        ),
        out_shape=[jax.ShapeDtypeStruct((rows, 2 * size), mine.dtype) for size in sizes],
        cost_estimate=pl.CostEstimate(flops=0, bytes_accessed=16 * rows * cols, transcendentals=0),
        name="unpack",
    )(core, mine, came)


def row_factor(values):
    return lax.rsqrt(jnp.mean(values * values, axis=-1, keepdims=True) + 1e-05)


def norm_backward(normed, factor, gain, grad):
    inner = grad * gain
    return factor * (inner - normed * jnp.mean(inner * normed, axis=-1, keepdims=True))


SWAP = [(0, 1), (1, 0)]


def swap(value, axis):
    return lax.ppermute(value, axis, SWAP)


def after(value, other):
    return lax.optimization_barrier((value, other))[0]


def by_core(mine, other):
    first = lax.axis_index("core") == 0
    return jnp.where(first, mine, other), jnp.where(first, other, mine)


def own_half(parts):
    return by_core(parts[0], parts[1])


def halves(value):
    size = value.shape[-1] // 2
    return value[..., :size], value[..., size:]


def chip_rows(parts):
    return joined_rows(*own_half(parts))


def joined_rows(mine, other):
    return jnp.concatenate(by_core(mine, swap(other, "core")), axis=0)


def wide_halves(value, size):
    return tuple(jnp.pad(part, ((0, 0), (0, size - part.shape[1]))) for part in halves(value))


class Ring:
    def __init__(self, chips):
        self.chips = chips
        order = list(range(0, chips, 2)) + list(range(chips - 1, 0, -2))
        after = order[1:] + order[:1]
        self.ahead, self.back = list(zip(order, after)), list(zip(after, order))
        me = lax.axis_index("chip")
        self.place = jnp.where(me % 2 == 0, me // 2, chips - 1 - me // 2)

    def chip_at(self, offset):
        place = (self.place + offset + self.chips) % self.chips
        return jnp.where(place < self.chips // 2, 2 * place, 2 * (self.chips - 1 - place) + 1)

    def gather(self, piece, joined, first=None, halved=True):
        rows = piece.shape[0]
        pieces, offsets = [piece], [0]
        up = down = piece
        steps = (self.chips - 1) // 2
        for step in range(1, steps + 1):
            up, down = lax.ppermute(up, "chip", self.ahead), lax.ppermute(down, "chip", self.back)
            up, down = lax.optimization_barrier((up, down))
            pieces += [up, down]
            offsets += [-step, step]
            if step == 1 and first is not None:
                first(up)
        far = self.chips // 2
        if not halved:
            pieces.append(lax.ppermute(up, "chip", self.ahead))
            return joined(pieces, [self.chip_at(offset) for offset in offsets + [far]])
        top = lax.ppermute(up[: rows // 2], "chip", self.ahead)
        bottom = lax.ppermute(down[rows // 2 :], "chip", self.back)
        pieces += lax.optimization_barrier((top, bottom))
        return joined(pieces, [self.chip_at(offset) for offset in offsets + [far]])

    def by_slices(self, pieces, places):
        rows, cols = pieces[0].shape
        full = jnp.zeros((self.chips, rows, cols), pieces[0].dtype)
        starts = [0] * (len(pieces) - 1) + [rows // 2]
        for value, place, start in zip(pieces, places + places[-1:], starts):
            full = lax.dynamic_update_slice(full, value[None], (place, start, 0))
        return full.reshape(-1, cols)

    def by_copies(self, pieces, places):
        rows, cols = pieces[0].shape
        count = len(pieces)

        def kernel(places_ref, *refs):
            out_ref, held, into, out = refs[count:]
            stages, results = [], []
            for at, ref in enumerate(refs[:count]):
                start = pl.multiple_of(places_ref[at] * rows, rows)
                slot = held.at[pl.ds(at * rows, rows), :]
                stages.append(pltpu.make_async_copy(ref, slot, into.at[at]))
                results.append(pltpu.make_async_copy(slot, out_ref.at[pl.ds(start, rows), :], out.at[at]))
                stages[-1].start()
            for stage, result in zip(stages, results):
                stage.wait()
                result.start()
            for result in results:
                result.wait()

        return pl.pallas_call(
            kernel,
            grid_spec=pltpu.PrefetchScalarGridSpec(
                num_scalar_prefetch=1,
                grid=(1,),
                in_specs=[pl.BlockSpec(memory_space=pl.ANY)] * count,
                out_specs=pl.BlockSpec(memory_space=pl.ANY),
                scratch_shapes=[pltpu.VMEM((self.chips * rows, cols), pieces[0].dtype)]
                + [pltpu.SemaphoreType.DMA((count,))] * 2,
            ),
            out_shape=jax.ShapeDtypeStruct((self.chips * rows, cols), pieces[0].dtype),
            cost_estimate=pl.CostEstimate(flops=0, bytes_accessed=4 * self.chips * rows * cols, transcendentals=0),
            name="lay_out",
        )(jnp.stack(places), *pieces)

    def scatter_sum(self, values):
        split = [value.reshape(self.chips, -1, value.shape[1]) for value in values]

        def join(offset, came=None):
            parts = [lax.dynamic_index_in_dim(value, self.chip_at(offset), 0, keepdims=False) for value in split]
            total = sum(part.astype(F32) for part in parts)
            return total if came is None else total + came.astype(F32)

        far = self.chips // 2
        up, down = join(far).astype(BF16), join(1 - far).astype(BF16)
        sent = []
        for step in range(far - 1, 0, -1):
            up, down = lax.ppermute(up, "chip", self.ahead), lax.ppermute(down, "chip", self.back)
            up, down = lax.optimization_barrier((up, down))
            up = join(step, up).astype(BF16)
            if step > 1:
                down = join(1 - step, down).astype(BF16)
            sent.append(up)
        last = lax.ppermute(up, "chip", self.ahead)
        return (lambda ready: join(0, after(down, ready)) + after(last, ready).astype(F32)), sent


def owner_rows(value):
    value = value.astype(F32)
    rows = value.shape[0] // 2
    mine, other = own_half((value[:rows], value[rows:]))
    return by_core(mine, swap(other, "core"))


def all_sum(value, axis, size):
    step = size // 2
    while step:
        came = lax.ppermute(value, axis, [(at, at ^ step) for at in range(size)])
        value = value + came
        step = step // 2
    return value


def local(chips, *args):
    return layer(chips, *args)


def layer(chips, tokens, norm_gain1, w_query, w_key, w_value, w_gate, w_decay, w_write, conv_query, conv_key,
          conv_value, a_log, dt_bias, out_gain, w_out, norm_gain2, w_ffgate, w_ffup, w_ffdown, cotangent):
    ring = Ring(chips)
    heads_n = a_log.shape[0] // 2
    ff = w_ffgate.shape[1] // 2
    tokens_o = swap(tokens, "tensor")
    cot_o = swap(cotangent, "tensor")

    pad = jnp.zeros((w_query.shape[0], 128 - 2 * heads_n), BF16)
    core = lax.axis_index("core").astype(jnp.int32).reshape(1)
    rates = jnp.concatenate(
        [part for pair in zip(*map(halves, (w_decay, w_write))) for part in (*pair, pad)], axis=1
    )
    mix_parts = pack(core, [w_out.T, w_query, w_key, w_value, w_gate, rates])
    ffn_rows = []

    def pack_ffn(ready):
        values = lax.optimization_barrier((w_ffgate, w_ffup, w_ffdown.T, ready))[:3]
        parts = [
            jnp.concatenate(parts, axis=1) for parts in zip(*(wide_halves(value, FF_HALF) for value in values))
        ]
        ffn_rows.append(chip_rows(parts))

    w_mix = [ring.gather(joined_rows(*mix_parts), ring.by_slices, pack_ffn)]
    w_mix.append(swap(w_mix[0], "core"))
    w_ffn = [ring.gather(after(ffn_rows[0], w_mix[0]), ring.by_copies, halved=False)]
    w_ffn.append(swap(w_ffn[0], "core"))
    val_w = heads_n * DV

    tokens32 = jnp.concatenate([tokens, tokens_o], axis=0).astype(F32)
    factor1 = row_factor(tokens32)
    unit1 = tokens32 * factor1
    normed1 = (unit1 * norm_gain1).astype(BF16)
    gain = out_gain.reshape(1, -1)
    params = []
    sides = [own_half(halves(value)) for value in (conv_query, conv_key, conv_value, a_log, dt_bias)]
    for cq, ck, cv, rate, bias in zip(*sides):
        heads_in = jnp.pad(jnp.stack([rate, bias]), ((0, 6), (0, 128 - heads_n)))
        params.append((cq, ck, cv, heads_in, gain))

    mixed = {}

    def mix(normed, seq, side):
        mixed[seq, side] = mix_forward(normed, w_mix[side], seq, params[side])

    mix(normed1, 1, 0)
    mix(after(normed1, mixed[1, 0][0]), 1, 1)
    part_o = out_rows((mixed[1, 0][0], mixed[1, 1][0]), w_mix, tokens.shape[1])
    came_s = swap(part_o, "tensor")
    mix(after(normed1, part_o), 0, 0)
    mix(after(normed1, mixed[0, 0][0]), 0, 1)
    gain2 = norm_gain2.reshape(1, -1)
    resid1, normed2_s = resid_rows_of((mixed[0, 0][0], mixed[0, 1][0]), w_mix, tokens, came_s, gain2)
    normed2_o = swap(normed2_s, "tensor")

    *units, part_s, back_s = ffn_both(normed2_s, cotangent, w_ffn[0], w_ffn[1], 0, 2 * LEN, F32)
    *units, part_low, back_low = ffn_both(normed2_o, cot_o, w_ffn[0], w_ffn[1], 1, 2 * LEN, BF16, units)
    came_rows2 = swap(back_low, "tensor")
    normed2, cot = (normed2_s, after(normed2_o, back_low)), (cotangent, cot_o)
    late_sent = late_grads(normed2, cot, units[3:])
    late_came = swap(late_sent, "core")
    late_own = late_grads((normed2_s, after(normed2_o, late_sent)), cot, units[:3])
    grad_resid, resid_s, grad_gain2 = resid_back(resid1, back_s, came_rows2, cotangent, gain2)
    resid_s = after(resid_s, late_own)
    resid_o = swap(resid_s, "tensor")
    resid_rows = (resid_s, resid_o)
    result = resid1 + part_s + swap(after(part_low, resid_o), "tensor").astype(F32)
    late_last, _ = ring.scatter_sum([late_own, late_came])

    cols = w_mix[0].shape[1] - val_w
    grad_proj, small = [None, None], [None, None]
    ready = late_own
    for step, (seq, side) in enumerate(((0, 1), (0, 0), (1, 1), (1, 0))):
        grad_proj[side], sums = mix_backward(
            after(resid_rows[seq], ready), w_mix[side], seq, params[side], mixed[seq, side][1:], cols,
            grad_proj[side]
        )
        ready = grad_proj[side]
        small[side] = sums if seq == 0 else small[side] + sums
        if step == 2:
            ready = mix_grads(resid_rows, (mixed[0, 1][0], mixed[1, 1][0]), normed1, grad_proj[1])
            mix_came = swap(ready, "core")
    mix_own = mix_grads(resid_rows, (mixed[0, 0][0], mixed[1, 0][0]), normed1, grad_proj[0], mix_came)
    mix_last, mix_sent = ring.scatter_sum([mix_own])
    late_sum = owner_rows(late_last(mix_own))
    grad_proj[0] = after(grad_proj[0], mix_own)

    _, back_sent, gain_o = back_rows(grad_proj, w_mix, unit1, 1)
    mix_rows = mix_last(back_sent)
    mine_rows, other_rows = own_half((mix_rows[: mix_rows.shape[0] // 2], mix_rows[mix_rows.shape[0] // 2 :]))
    key_w = heads_n * DK
    mix_sum = unpack(core, mine_rows, swap(other_rows, "core"), (val_w, key_w, key_w, val_w, val_w, 128))
    back_s, _, gain_s = back_rows(grad_proj, w_mix, unit1, 0)
    grad_gain1 = gain_o[0] + gain_s[0]
    came_back = swap(back_sent, "tensor")
    last_parts = (came_back, back_s, unit1[:LEN], factor1[:LEN])
    came_back, back_s, unit_s, factor_s, *_ = lax.optimization_barrier((*last_parts, *mix_sent[-1:]))
    grad_rows1 = back_s + came_back.astype(F32)
    grad_tokens = grad_resid + norm_backward(unit_s, factor_s, norm_gain1, grad_rows1)

    head_rows = jnp.concatenate(by_core(small[0][0], small[1][0]), axis=0)
    out_gain_row = jnp.sum(head_rows[:, 8], axis=0, keepdims=True)
    wide = jnp.concatenate(
        [grad_gain1.reshape(-1, DV), grad_gain2.reshape(-1, DV), out_gain_row, head_rows.reshape(-1, DV)], axis=0
    )
    wide = all_sum(all_sum(wide, "chip", chips), "core", 2)
    count = grad_gain1.shape[0] // DV
    gains = all_sum(wide[: 2 * count + 1], "tensor", 2)
    head_rows = wide[2 * count + 1 :].reshape(2 * heads_n, 16, DV)

    def taps(rows):
        return jnp.transpose(rows, (1, 0, 2)).reshape(4, -1)

    def columns(parts, start, size):
        return jnp.concatenate([part[:, start : start + size] for part in parts], axis=1)

    return (
        result.astype(BF16),
        grad_tokens,
        gains[:count].reshape(-1),
        mix_sum[1],
        mix_sum[2],
        mix_sum[3],
        mix_sum[4],
        jnp.concatenate([mix_sum[5][:, start : start + heads_n] for start in (0, 128)], axis=1),
        jnp.concatenate([mix_sum[5][:, start : start + heads_n] for start in (heads_n, 128 + heads_n)], axis=1),
        taps(head_rows[:, 4:8, :DK]),
        taps(head_rows[:, 4:8, DK:]),
        taps(head_rows[:, :4]),
        head_rows[:, 9, 0],
        head_rows[:, 9, 1],
        gains[2 * count],
        mix_sum[0].T,
        gains[count : 2 * count].reshape(-1),
        columns(late_sum, 0, ff),
        columns(late_sum, FF_HALF, ff),
        columns(late_sum, 2 * FF_HALF, ff).T,
    )


def solution(mesh):
    chips = mesh.shape["dp"] // 2
    inner = jax.sharding.Mesh(mesh.devices.reshape(chips, 2, -1), ("chip", "core", "tensor"))
    dp, rows, every = ("chip", "core"), P(("chip", "core", "tensor"), None), P()
    down, across, taps, head = P(dp, "tensor"), P("tensor", dp), P(None, "tensor"), P("tensor")
    return jax.shard_map(
        functools.partial(local, chips),
        mesh=inner,
        in_specs=(rows, every, down, down, down, down, down, down, taps, taps, taps, head, head, every, across, every,
                  down, down, across, rows),
        out_specs=(rows, rows, every, down, down, down, down, down, down, taps, taps, taps, head, head, every, across,
                   every, down, down, across),
        check_vma=False,
    )
```
